32 devices in a mesh: dp: 2 (over x), ctx: 4 (over z), tp: 4 (over y, core).
Axes of the slice: x: 2, y: 2, z: 4, core: 2. Of those that a mesh axis runs over, the one named last changes fastest.
Arguments:
- inputs: bfloat16 [4, 2048, 768], P('dp', 'ctx'), may hold values from -6 to 6
- segment_ids: int32 [4, 2048], P('dp'), may hold values from 0 to 15, never falling along the last dimension, each value on 1 to 1536 neighbouring positions
- w_query: bfloat16 [768, 768], P('dp', 'tp'), may hold values from -0.3125 to 0.3125
- w_key: bfloat16 [768, 768], P('dp', 'tp'), may hold values from -0.3125 to 0.3125
- w_value: bfloat16 [768, 768], P('dp', 'tp'), may hold values from -0.21875 to 0.21875
- w_output: bfloat16 [768, 768], P('tp', 'dp'), may hold values from -0.875 to 0.875
- w_inner: bfloat16 [768, 3072], P('dp', 'tp'), may hold values from -0.21875 to 0.21875
- w_outer: bfloat16 [3072, 768], P('tp', 'dp'), may hold values from -0.109375 to 0.109375
- gain_attn: float32 [768], replicated, may hold values from 0.1 to 1.9
- shift_attn: float32 [768], replicated, may hold values from -3 to 3
- gain_ffn: float32 [768], replicated, may hold values from 0.1 to 1.9
- shift_ffn: float32 [768], replicated, may hold values from -3 to 3
- cotangent: bfloat16 [4, 2048, 768], P('dp', 'ctx'), may hold values from -6 to 6
Outputs:
- outputs: bfloat16 [4, 2048, 768], P('dp', 'ctx')
- input_grad: bfloat16 [4, 2048, 768], P('dp', 'ctx')
- grad_w_query: float32 [768, 768], P('dp', 'tp')
- grad_w_key: float32 [768, 768], P('dp', 'tp')
- grad_w_value: float32 [768, 768], P('dp', 'tp')
- grad_w_output: float32 [768, 768], P('tp', 'dp')
- grad_w_inner: float32 [768, 3072], P('dp', 'tp')
- grad_w_outer: float32 [3072, 768], P('tp', 'dp')
- grad_gain_attn: float32 [768], replicated
- grad_shift_attn: float32 [768], replicated
- grad_gain_ffn: float32 [768], replicated
- grad_shift_ffn: float32 [768], replicated
The draws below stay inside these ranges and needn't reach their ends.
Inputs may be any that keep to these rules, and one draw needn't show every extreme that they name: `segment_ids`: along each sequence the document numbers never fall; each of the 16 numbers appears in every sequence, in 1 to 1536 positions, and one of them in exactly 1536.
All inputs are finite; a program needn't handle non-finite values.
Results may differ from the reference program's by a relative error of at most 0.02.
Values may be sent and summed in bfloat16 or wider, within the bound.
No kernel may reach another device: no remote copies, remote signals or barrier semaphores. Data moves between devices by JAX's collectives and lax.ppermute only.
A program may use at most 128 MiB of HBM per device.

```python
import math
import jax
import jax.numpy as jnp
import numpy as np
from jax import lax

D = 768
HEADS = 12
HEAD_DIM = 64
FF = 3072
LEN = 2048
DOCS = 16
MOST = 1536
SEQS = 4


def level_of(key, extent, cuts, low, top_value):
    def one(axis_at, blocks):
        heights = jax.random.uniform(jax.random.fold_in(jax.random.fold_in(key, 6), axis_at), (blocks,), jnp.float32, low / len(cuts), top_value / len(cuts))
        return jnp.repeat(jnp.exp(heights), extent[axis_at] // blocks).reshape((-1,) + (1,) * (len(extent) - axis_at - 1))

    loudness = one(*cuts[0])
    for cut in cuts[1:]:
        loudness = loudness * one(*cut)
    return loudness


def profile(number_of, total, limit, slope):
    weights = [(1 << 20) // math.isqrt(standing ** slope) + 1 for standing in range(2, number_of + 1)]
    spare, given = total - limit - (number_of - 1), [1] * (number_of - 1)
    while spare > 0:
        movable = [i for i in range(number_of - 1) if given[i] < limit]
        pool, left = sum([weights[i] for i in movable]), spare
        for i in movable:
            addition = min(limit - given[i], max(1, left * weights[i] // pool), spare)
            given[i] = given[i] + addition
            spare = spare - addition
    return np.array([limit] + given)


def uneven(own_key, amount, total, bound, skew):
    if amount == 2:
        one = jax.random.randint(own_key, (), max(1, total - bound), min(bound, total - 1) + 1)
        return jnp.stack([one, total - one])
    sizes = jnp.asarray(profile(amount, total, bound, skew), jnp.int32)
    pairs = (amount - 1) // 2
    donor, taker = sizes[1:1 + 2 * pairs:2], sizes[2:2 + 2 * pairs:2]
    room = jnp.minimum(donor - 1, bound - taker)
    passed = jax.random.randint(jax.random.fold_in(own_key, 1), (pairs,), 0, 1 << 20) % (room + 1)
    sizes = sizes.at[1:1 + 2 * pairs:2].set(donor - passed).at[2:2 + 2 * pairs:2].set(taker + passed)
    return sizes[jax.random.permutation(jax.random.fold_in(own_key, 2), amount)]


def noise(rng, shape, scale, reach, split=(), kind=jnp.bfloat16):
    values = jax.random.normal(rng, shape, jnp.float32) * scale
    if len(split) > 0:
        values = level_of(rng, shape, split, -0.22, 0.18) * values
    return jnp.clip(values, min=-reach, max=reach).astype(kind)


def setup_inputs(seed: int = 0) -> dict:
    streams_of = jax.random.split(jax.random.key(seed), 14)
    return {
        "inputs": noise(streams_of[0], (SEQS, LEN, D), 1.0, 6.0, ((0, 2), (1, 4))),
        "segment_ids": jax.vmap(lambda own: jnp.searchsorted(jnp.cumsum(uneven(own, DOCS, LEN, MOST, 2)), jnp.arange(LEN), side="right"))(jax.random.split(streams_of[1], SEQS)).reshape((SEQS, LEN)).astype(jnp.int32),
        "w_query": noise(streams_of[2], (D, D), (D // 2) ** -0.5, 0.3125, ((0, 2), (1, 4))),
        "w_key": noise(streams_of[3], (D, D), (D // 2) ** -0.5, 0.3125, ((0, 2), (1, 4))),
        "w_value": noise(streams_of[4], (D, D), D ** -0.5, 0.21875, ((0, 2), (1, 4))),
        "w_output": noise(streams_of[5], (D, D), (D // 16) ** -0.5, 0.875, ((0, 4), (1, 2))),
        "w_inner": noise(streams_of[6], (D, FF), D ** -0.5, 0.21875, ((0, 2), (1, 4))),
        "w_outer": noise(streams_of[7], (FF, D), FF ** -0.5, 0.109375, ((0, 4), (1, 2))),
        "gain_attn": jnp.clip(1.0 + 0.18 * jax.random.normal(streams_of[8], (D,), jnp.float32), 0.1, 1.9),
        "shift_attn": noise(streams_of[9], (D,), 0.5, 3.0, (), jnp.float32),
        "gain_ffn": jnp.clip(1.0 + 0.18 * jax.random.normal(streams_of[10], (D,), jnp.float32), 0.1, 1.9),
        "shift_ffn": noise(streams_of[11], (D,), 0.5, 3.0, (), jnp.float32),
        "cotangent": noise(streams_of[12], (SEQS, LEN, D), 1.0, 6.0, ((0, 2), (1, 4))),
    }


EPSILON = 1e-06
MASKED = -1e+30

@jax.custom_vjp
def low(v):
    return lax.optimization_barrier(v.astype(jnp.bfloat16)).astype(jnp.float32)

@jax.custom_vjp
def low_back(v):
    return v

def low_keep(v):
    return (low(v), None)

def low_pass(kept, grad):
    return (grad,)

def back_keep(v):
    return (v, None)

def back_low(kept, grad):
    return (low(grad),)
low.defvjp(low_keep, low_pass)
low_back.defvjp(back_keep, back_low)

def matmul(left_side, right_side):
    return jnp.dot(left_side, right_side, precision=lax.Precision.HIGHEST)

def layer_norm(token_rows, norm_gain, norm_shift):
    centre = lax.optimization_barrier(jnp.mean(token_rows, axis=-1, keepdims=True))
    centred = token_rows - centre
    spread = lax.optimization_barrier(jnp.mean(centred * centred, axis=-1, keepdims=True))
    return centred * lax.rsqrt(spread + EPSILON) * norm_gain + norm_shift

def rotary_tables(segments):
    length = segments.shape[-1]
    index_row = jnp.arange(length, dtype=jnp.int32)
    starts = jnp.concatenate([jnp.ones(segments.shape[:-1] + (1,), jnp.bool_), segments[..., 1:] != segments[..., :-1]], axis=-1)
    first_pos = lax.cummax(jnp.where(starts, index_row, jnp.zeros_like(index_row)), axis=segments.ndim - 1)
    position = (index_row - first_pos).astype(jnp.float32)
    half_width = HEAD_DIM // 2
    theta = jnp.power(10000.0, -2.0 * jnp.arange(half_width, dtype=jnp.float32) / HEAD_DIM)
    angle = position[..., None] * theta
    return (jnp.cos(angle)[..., None, :], jnp.sin(angle)[..., None, :])

def rotate(head_rows, cosines, sine_values):
    half_width = head_rows.shape[-1] // 2
    leading = head_rows[..., :half_width]
    trailing = head_rows[..., half_width:]
    return jnp.concatenate([leading * cosines - trailing * sine_values, trailing * cosines + leading * sine_values], axis=-1)

def sequence_forward(token_in, params, cosines, sine_values, same_doc):
    w_query, w_key, w_value, w_output, w_inner, w_outer, gain_attn, shift_attn, gain_ffn, shift_ffn = params
    head_shape = (LEN, HEADS, HEAD_DIM)
    q_lin = low_back(matmul(token_in, w_query)).reshape(head_shape)
    k_lin = low_back(matmul(token_in, w_key)).reshape(head_shape)
    queries = low(rotate(q_lin, cosines, sine_values))
    key_heads = low(rotate(k_lin, cosines, sine_values))
    values = low(low_back(matmul(token_in, w_value))).reshape(head_shape)
    block_rows = min(512, LEN)
    factor = 1.0 / math.sqrt(HEAD_DIM)

    def attend(sliced):
        query_block, same_block = sliced
        scores = low_back(factor * jnp.einsum('qhe,khe->hqk', query_block, key_heads, precision=lax.Precision.HIGHEST))
        scores = jnp.where(same_block[None], scores, MASKED)
        row_max = lax.optimization_barrier(jnp.max(scores, axis=-1, keepdims=True))
        exponent = jnp.exp(scores - row_max)
        probs = low(exponent / lax.optimization_barrier(jnp.sum(exponent, axis=-1, keepdims=True)))
        return jnp.einsum('hqk,khe->qhe', probs, values, precision=lax.Precision.HIGHEST)
    mixed = lax.map(jax.checkpoint(attend), (queries.reshape(LEN // block_rows, block_rows, HEADS, HEAD_DIM), same_doc.reshape(LEN // block_rows, block_rows, LEN)))
    mixed = low(low_back(mixed.reshape(LEN, D)))
    attended = low_back(matmul(mixed, w_output))
    first = layer_norm(token_in + attended, gain_attn, shift_attn)
    inner = low_back(matmul(low(first), w_inner))
    active = low(jax.nn.gelu(inner, approximate=False))
    feed = low_back(matmul(active, w_outer))
    return layer_norm(first + feed, gain_ffn, shift_ffn)

def reference(inputs, segment_ids, w_query, w_key, w_value, w_output, w_inner, w_outer, gain_attn, shift_attn, gain_ffn, shift_ffn, cotangent):
    params = (w_query.astype(jnp.float32), w_key.astype(jnp.float32), w_value.astype(jnp.float32), w_output.astype(jnp.float32), w_inner.astype(jnp.float32), w_outer.astype(jnp.float32), gain_attn, shift_attn, gain_ffn, shift_ffn)

    def one_sequence(totals, sliced):
        token_rows, segments, grad_rows = sliced
        cosines, sine_values = rotary_tables(segments)
        same_doc = segments[:, None] == segments[None, :]

        def forward(token_in, weight_set):
            return sequence_forward(token_in, weight_set, cosines, sine_values, same_doc)
        result, pullback = jax.vjp(forward, token_rows.astype(jnp.float32), params)
        grad_in, grad_params = pullback(grad_rows.astype(jnp.float32))
        totals = jax.tree.map(lambda left_side, right_side: left_side + right_side, totals, grad_params)
        return (totals, (result.astype(jnp.bfloat16), grad_in.astype(jnp.bfloat16)))
    zero_grads = jax.tree.map(jnp.zeros_like, params)
    totals, (outputs, input_grad) = lax.scan(one_sequence, zero_grads, (inputs, segment_ids, cotangent))
    return (outputs, input_grad, totals[0], totals[1], totals[2], totals[3], totals[4], totals[5], totals[6], totals[7], totals[8], totals[9])
```

```python
import functools
import math

import jax
import jax.numpy as jnp
from jax import lax
from jax.experimental import pallas as pl
from jax.experimental.pallas import tpu as pltpu
from jax.sharding import PartitionSpec as P

HEAD_DIM = 64
HALF = HEAD_DIM // 2
DOCS = 16
EPSILON = 1e-06
MASKED = -1e30
F32 = jnp.float32
BF16 = jnp.bfloat16
GROUP = 4
KEY_BLOCKS = 8


def dot(left, right, left_dim, right_dim):
    return lax.dot_general(
        left, right, (((left_dim,), (right_dim,)), ((), ())), preferred_element_type=F32
    )


def swap(value, axis, k, size=GROUP):
    return lax.ppermute(value, axis, [(i, i ^ k) for i in range(size)])


def pick(stack, index):
    return lax.dynamic_index_in_dim(stack, index, 0, keepdims=False)


def split_bit(value, bit, axis=0):
    half = value.shape[axis] // 2
    keep = lax.dynamic_slice_in_dim(value, bit * half, half, axis)
    send = lax.dynamic_slice_in_dim(value, (1 - bit) * half, half, axis)
    return keep, send


def join_bit(own, other, bit, axis=0):
    low = jnp.where(bit == 0, own, other)
    high = jnp.where(bit == 0, other, own)
    return jnp.concatenate([low, high], axis)


def block_mask(base, span_ref, shape):
    key_index = base + lax.broadcasted_iota(jnp.int32, shape, 0)
    return (key_index >= span_ref[0, 0:1, :]) & (key_index < span_ref[0, 1:2, :])


def attend_kernel(flags, bases, q_ref, k_ref, v_ref, span_ref, o_ref, lse_ref, m_s, l_s, acc_s):
    i = pl.program_id(0)
    heads = q_ref.shape[1] // HEAD_DIM
    rows = q_ref.shape[2]
    m_s[...] = jnp.full(m_s.shape, MASKED, F32)
    l_s[...] = jnp.zeros(l_s.shape, F32)
    acc_s[...] = jnp.zeros(acc_s.shape, F32)

    def work(j, masked):
        ok = block_mask(bases[j], span_ref, (rows, rows)) if masked else None
        for h in range(heads):
            part = slice(h * HEAD_DIM, (h + 1) * HEAD_DIM)
            scores = dot(k_ref[j, part, :], q_ref[0, part, :], 0, 0)
            if masked:
                scores = jnp.where(ok, scores, MASKED)
            old = m_s[h : h + 1, :]
            new = jnp.maximum(old, jnp.max(scores, axis=0, keepdims=True))
            probs = jnp.exp(scores - new)
            alpha = jnp.exp(old - new)
            m_s[h : h + 1, :] = new
            l_s[h : h + 1, :] = l_s[h : h + 1, :] * alpha + jnp.sum(probs, axis=0, keepdims=True)
            acc_s[part, :] = acc_s[part, :] * alpha + dot(
                v_ref[j, part, :], probs.astype(BF16), 1, 0
            )

    def step(j, carry):
        flag = flags[i * KEY_BLOCKS + j]

        @pl.when(flag == 1)
        def _():
            work(j, True)

        @pl.when(flag == 2)
        def _():
            work(j, False)

        return carry

    lax.fori_loop(0, KEY_BLOCKS, step, 0)
    for h in range(heads):
        part = slice(h * HEAD_DIM, (h + 1) * HEAD_DIM)
        total = l_s[h : h + 1, :]
        o_ref[0, part, :] = (acc_s[part, :] / total).astype(BF16)
        lse_ref[0, h : h + 1, :] = m_s[h : h + 1, :] + jnp.log(total)


def attend(flags, bases, q, k, v, span):
    blocks, width, rows = q.shape
    heads = width // HEAD_DIM
    one = lambda shape: pl.BlockSpec((1,) + shape, lambda i, *_: (i, 0, 0))
    whole = pl.BlockSpec(k.shape, lambda i, *_: (0, 0, 0))
    return pl.pallas_call(
        attend_kernel,
        grid_spec=pltpu.PrefetchScalarGridSpec(
            num_scalar_prefetch=2,
            grid=(blocks,),
            in_specs=[one((width, rows)), whole, whole, one((2, rows))],
            out_specs=[one((width, rows)), one((heads, rows))],
            scratch_shapes=[
                pltpu.VMEM((8, rows), F32),
                pltpu.VMEM((8, rows), F32),
                pltpu.VMEM((width, rows), F32),
            ],
        ),
        out_shape=[
            jax.ShapeDtypeStruct(q.shape, BF16),
            jax.ShapeDtypeStruct((blocks, heads, rows), F32),
        ],
        name="attend",
    )(flags, bases, q, k, v, span)


def attend_back_kernel(
    flags, bases, q_ref, k_ref, v_ref, span_ref, o_ref, d_ref, lse_ref,
    dq_ref, own_k_ref, own_v_ref, far_k_ref, far_v_ref, dk_s, dv_s, delta_s,
):
    i = pl.program_id(0)
    heads = q_ref.shape[1] // HEAD_DIM
    rows = q_ref.shape[2]

    @pl.when(i == 0)
    def _():
        dk_s[...] = jnp.zeros(dk_s.shape, F32)
        dv_s[...] = jnp.zeros(dv_s.shape, F32)

    dq_ref[...] = jnp.zeros(dq_ref.shape, F32)
    for h in range(heads):
        part = slice(h * HEAD_DIM, (h + 1) * HEAD_DIM)
        delta_s[h : h + 1, :] = jnp.sum(
            o_ref[0, part, :].astype(F32) * d_ref[0, part, :].astype(F32), axis=0, keepdims=True
        )

    def work(j, masked):
        ok = block_mask(bases[j], span_ref, (rows, rows)) if masked else None
        for h in range(heads):
            part = slice(h * HEAD_DIM, (h + 1) * HEAD_DIM)
            key, query, grad = k_ref[j, part, :], q_ref[0, part, :], d_ref[0, part, :]
            scores = dot(key, query, 0, 0)
            probs = jnp.exp(scores - lse_ref[0, h : h + 1, :])
            if masked:
                probs = jnp.where(ok, probs, 0.0)
            grad_probs = dot(v_ref[j, part, :], grad, 0, 0)
            grad_scores = (probs * (grad_probs - delta_s[h : h + 1, :])).astype(BF16)
            dv_s[j, part, :] += dot(grad, probs.astype(BF16), 1, 1)
            dk_s[j, part, :] += dot(query, grad_scores, 1, 1)
            dq_ref[0, part, :] += dot(key, grad_scores, 1, 0)

    def step(j, carry):
        flag = flags[i * KEY_BLOCKS + j]

        @pl.when(flag == 1)
        def _():
            work(j, True)

        @pl.when(flag == 2)
        def _():
            work(j, False)

        return carry

    lax.fori_loop(0, KEY_BLOCKS, step, 0)

    @pl.when(i == pl.num_programs(0) - 1)
    def _():
        own = own_k_ref.shape[0]
        own_k_ref[...] = dk_s[:own]
        own_v_ref[...] = dv_s[:own]
        far_k_ref[...] = dk_s[own:].astype(BF16)
        far_v_ref[...] = dv_s[own:].astype(BF16)


def attend_back(flags, bases, q, k, v, span, o, grad, lse):
    blocks, width, rows = q.shape
    heads = width // HEAD_DIM
    one = lambda shape: pl.BlockSpec((1,) + shape, lambda i, *_: (i, 0, 0))
    whole = pl.BlockSpec(k.shape, lambda i, *_: (0, 0, 0))
    half = pl.BlockSpec(q.shape, lambda i, *_: (0, 0, 0))
    return pl.pallas_call(
        attend_back_kernel,
        grid_spec=pltpu.PrefetchScalarGridSpec(
            num_scalar_prefetch=2,
            grid=(blocks,),
            in_specs=[
                one((width, rows)), whole, whole, one((2, rows)),
                one((width, rows)), one((width, rows)), one((heads, rows)),
            ],
            out_specs=[one((width, rows)), half, half, half, half],
            scratch_shapes=[
                pltpu.VMEM(k.shape, F32),
                pltpu.VMEM(k.shape, F32),
                pltpu.VMEM((8, rows), F32),
            ],
        ),
        out_shape=[
            jax.ShapeDtypeStruct(q.shape, F32),
            jax.ShapeDtypeStruct(q.shape, F32),
            jax.ShapeDtypeStruct(q.shape, F32),
            jax.ShapeDtypeStruct(q.shape, BF16),
            jax.ShapeDtypeStruct(q.shape, BF16),
        ],
        name="attend_back",
    )(flags, bases, q, k, v, span, o, grad, lse)


def rotate(value, cosines, sines):
    rows = value.shape[-1]
    parts = value.reshape(-1, 2, HALF, rows)
    lead, trail = parts[:, 0], parts[:, 1]
    return jnp.stack(
        [lead * cosines - trail * sines, trail * cosines + lead * sines], axis=1
    ).reshape(value.shape)


def norm_stats(rows):
    centre = jnp.mean(rows, axis=-1, keepdims=True)
    centred = rows - centre
    spread = jnp.mean(centred * centred, axis=-1, keepdims=True)
    scale = lax.rsqrt(spread + EPSILON)
    return centred * scale, scale


def norm_back(grad, normal, scale, gain):
    dn = grad * gain
    return scale * (
        dn
        - jnp.mean(dn, axis=-1, keepdims=True)
        - normal * jnp.mean(dn * normal, axis=-1, keepdims=True)
    )


def per_device(
    dp_size, inputs, segment_ids, w_query, w_key, w_value, w_output, w_inner, w_outer,
    gain_attn, shift_attn, gain_ffn, shift_ffn, cotangent,
):
    seqs, local_rows, width = inputs.shape
    rows = local_rows // 2
    x = lax.axis_index("dp")
    z = lax.axis_index("ctx")
    t = lax.axis_index("tp")
    y, c = t // 2, t % 2
    pair = dp_size == 2
    head_cols = w_query.shape[1]
    half_width = width // 2

    def turn(value):
        if not pair:
            return value
        own, other = split_bit(value, x, value.ndim - 1)
        return jnp.concatenate([own, other], value.ndim - 1)

    def gather(local, axis):
        if not pair:
            near = lax.all_gather(local, "dp", axis=axis, tiled=True)
            return near, swap(near, "tp", 2)
        cut = local.shape[0] // 2
        across_x = swap(local, "dp", 1, 2)
        across_y = swap(local, "tp", 2)
        corner = jnp.concatenate(
            [swap(across_x[:cut], "tp", 2), swap(across_y[cut:], "dp", 1, 2)], 0
        )
        return (
            jnp.concatenate([local, across_x], axis),
            jnp.concatenate([across_y, corner], axis),
        )

    def reduce_dp(value, axis, first):
        if not pair:
            return lax.psum_scatter(
                value.astype(BF16), "dp", scatter_dimension=axis, tiled=True
            ).astype(F32)
        half = value.shape[axis] // 2
        keep = lax.slice_in_dim(value, 0, half, axis=axis)
        send = lax.slice_in_dim(value, half, 2 * half, axis=axis)
        return keep.astype(F32) + swap(send.astype(BF16), "dp", 1, 2).astype(F32)

    def reduce_ctx(value):
        bit0, bit1 = z % 2, z // 2
        keep, send = split_bit(value.astype(BF16), bit0)
        keep = keep.astype(F32) + swap(send, "ctx", 1).astype(F32)
        keep, send = split_bit(keep, bit1)
        keep = (keep + swap(send.astype(BF16), "ctx", 2).astype(F32)).astype(BF16)
        keep = join_bit(keep, swap(keep, "ctx", 2), bit1)
        return join_bit(keep, swap(keep, "ctx", 1), bit0).astype(F32)

    def own_tokens(value):
        return lax.dynamic_slice(value, (y, c * rows, 0), (1, rows, value.shape[2]))[0]

    own_in = turn(own_tokens(inputs))
    in_1 = swap(own_in, "ctx", 1)
    in_2 = swap(own_in, "ctx", 2)
    in_blocks = [own_in, in_1, in_2, swap(in_2, "ctx", 1)]
    own_cot = turn(own_tokens(cotangent)).astype(F32)
    gain_a, shift_a, gain_f, shift_f = [
        turn(v)[None, :] for v in (gain_attn, shift_attn, gain_ffn, shift_ffn)
    ]

    near, far = gather(jnp.concatenate([w_query, w_key, w_value], 1), 0)
    stack = jnp.stack([near, swap(near, "tp", 1), far, swap(far, "tp", 1)])
    w_qkv = [pick(stack, (t ^ z) ^ k) for k in range(GROUP)]
    near, far = gather(w_output, 1)
    stack = jnp.stack([near, swap(near, "tp", 1), far, swap(far, "tp", 1)])
    w_out = [pick(stack, (t ^ z) ^ k) for k in range(GROUP)]
    w_in = jnp.concatenate(gather(w_inner, 0), 1)
    w_up = jnp.concatenate(gather(w_outer, 1), 0)

    docs = pick(segment_ids, y)
    doc_names = jnp.arange(DOCS, dtype=jnp.int32)[:, None]
    doc_start = jnp.sum((docs[None, :] < doc_names).astype(jnp.int32), 1)
    doc_end = jnp.sum((docs[None, :] <= doc_names).astype(jnp.int32), 1)
    doc_blocks = docs.reshape(GROUP, 2, rows)
    order = jnp.stack([z ^ k for k in range(GROUP)])
    query_docs = jnp.stack([doc_blocks[z ^ k, c] for k in range(GROUP)])
    far_docs = jnp.stack([doc_blocks[z ^ k, 1 - c] for k in range(GROUP)])
    hot = query_docs[:, None, :] == doc_names[None]
    starts = jnp.sum(jnp.where(hot, doc_start[None, :, None], 0), 1)
    ends = jnp.sum(jnp.where(hot, doc_end[None, :, None], 0), 1)
    span = jnp.stack([starts, ends], 1)
    query_bases = (order * 2 + c) * rows
    bases = jnp.concatenate([query_bases, (order * 2 + 1 - c) * rows])
    key_docs = jnp.concatenate([query_docs, far_docs])
    key_low, key_high = key_docs[:, 0], key_docs[:, -1]
    low, high = query_docs[:, :1], query_docs[:, -1:]
    meets = (low <= key_high[None]) & (key_low[None] <= high)
    one_doc = (low == high) & (key_low == low) & (key_high == low)
    flags = jnp.where(meets, jnp.where(one_doc, 2, 1), 0).astype(jnp.int32).reshape(-1)
    position = (
        query_bases[:, None] + jnp.arange(rows, dtype=jnp.int32)[None] - starts
    ).astype(F32)
    theta = jnp.power(10000.0, -2.0 * jnp.arange(HALF, dtype=F32) / HEAD_DIM)
    angle = position[:, None, :] * theta[None, :, None]
    cosines, sines = jnp.cos(angle), jnp.sin(angle)

    factor = 1.0 / math.sqrt(HEAD_DIM)
    queries, keys, values, far_keys, far_values = [], [], [], [], []
    for k, block in enumerate(in_blocks):
        lin = dot(w_qkv[0], block, 0, 1)
        query = rotate(lin[:head_cols], cosines[k], sines[k]).astype(BF16) * BF16(factor)
        key = rotate(lin[head_cols : 2 * head_cols], cosines[k], sines[k]).astype(BF16)
        value = lin[2 * head_cols :].astype(BF16)
        both = swap(jnp.stack([key, value]), "tp", 1)
        queries.append(query)
        keys.append(key)
        values.append(value)
        far_keys.append(both[0])
        far_values.append(both[1])
    queries = jnp.stack(queries)
    keys = jnp.stack(keys + far_keys)
    values = jnp.stack(values + far_values)

    mixed, lse = attend(flags, bases, queries, keys, values, span)
    own_mixed = [mixed[0]] + [swap(mixed[k], "ctx", k) for k in range(1, GROUP)]
    attended = functools.reduce(
        jnp.add, [dot(own_mixed[k], w_out[k], 0, 0) for k in range(GROUP)]
    )

    normal_a, scale_a = norm_stats(own_in.astype(F32) + attended)
    first = normal_a * gain_a + shift_a
    first_own = first.astype(BF16)
    first_low = jnp.concatenate([first_own, swap(first_own, "tp", 1)])
    inner = dot(first_low, w_in, 1, 0)
    active, active_back = jax.vjp(functools.partial(jax.nn.gelu, approximate=False), inner)
    active = active.astype(BF16)
    feed = dot(active, w_up, 1, 0)
    feed = feed[:rows] + swap(feed[rows:], "tp", 1)
    normal_f, scale_f = norm_stats(first + feed)
    second = (normal_f * gain_f + shift_f).astype(BF16)

    d_second = norm_back(own_cot, normal_f, scale_f, gain_f)
    d_feed_own = d_second.astype(BF16)
    d_feed = jnp.concatenate([d_feed_own, swap(d_feed_own, "tp", 1)])
    d_active = dot(d_feed, w_up, 1, 1)
    d_inner = active_back(d_active)[0].astype(BF16)
    grad_up = dot(active, d_feed, 0, 0)
    grad_in = dot(first_low, d_inner, 0, 0)
    hidden = dot(d_inner, w_in, 1, 1)
    d_first = d_second + hidden[:rows] + swap(hidden[rows:], "tp", 1)
    d_resid = norm_back(d_first, normal_a, scale_a, gain_a)
    d_attended = d_resid.astype(BF16)

    d_mixed = [dot(w_out[k], d_attended, 1, 1).astype(BF16) for k in range(GROUP)]
    d_mixed = jnp.stack([d_mixed[0]] + [swap(d_mixed[k], "ctx", k) for k in range(1, GROUP)])
    d_query, d_key, d_value, sent_key, sent_value = attend_back(
        flags, bases, queries, keys, values, span, mixed, d_mixed, lse
    )
    sibling = swap(jnp.stack([sent_key, sent_value]), "tp", 1).astype(F32)
    d_key = d_key + sibling[0]
    d_value = d_value + sibling[1]
    d_lin = []
    for k in range(GROUP):
        d_lin.append(
            jnp.concatenate(
                [
                    rotate(d_query[k] * factor, cosines[k], -sines[k]).astype(BF16),
                    rotate(d_key[k], cosines[k], -sines[k]).astype(BF16),
                    d_value[k].astype(BF16),
                ]
            )
        )
    own_lin = [d_lin[0]] + [swap(d_lin[k], "ctx", k) for k in range(1, GROUP)]
    through = functools.reduce(
        jnp.add, [dot(own_lin[k], w_qkv[k], 0, 1) for k in range(GROUP)]
    )
    input_own = (d_resid + through).astype(BF16)

    def spread(value):
        value = turn(value)
        a = jnp.stack([value, swap(value, "tp", 1)])
        b = swap(a, "tp", 2)
        quad = jnp.concatenate([a, b])
        parts = [pick(quad, (k ^ t)) for k in range(GROUP)]
        return jnp.stack(parts).reshape(seqs, local_rows, width)

    outputs = spread(second)
    input_grad = spread(input_own)

    hidden_cut = grad_up.shape[0] // 2
    keep, send = grad_up[:hidden_cut], grad_up[hidden_cut:]
    part_up = reduce_dp(keep + swap(send.astype(BF16), "tp", 2).astype(F32), 1, False)
    shard_up = reduce_ctx(part_up)
    part_in = reduce_dp(grad_in, 0, True)
    keep, send = part_in[:, :hidden_cut], part_in[:, hidden_cut:]
    part_in = keep + swap(send.astype(BF16), "tp", 2).astype(F32)
    shard_in = reduce_ctx(part_in)

    grad_out = jnp.stack([dot(own_mixed[k], d_attended, 1, 0) for k in range(GROUP)])
    ordered = [pick(grad_out, (t ^ z) ^ k) for k in range(GROUP)]
    got = swap(jnp.stack([ordered[1], ordered[3]]).astype(BF16), "tp", 1).astype(F32)
    keep = ordered[0] + got[0]
    send = ordered[2] + got[1]
    part_out = reduce_dp(keep + swap(send.astype(BF16), "tp", 2).astype(F32), 1, False)
    shard_out = reduce_ctx(part_out)

    grad_qkv = functools.reduce(
        jnp.add, [dot(in_blocks[k], d_lin[k], 0, 1) for k in range(GROUP)]
    )
    part_qkv = reduce_dp(grad_qkv, 0, True)
    pieces = part_qkv.reshape(2, 2, part_qkv.shape[0] // GROUP, part_qkv.shape[1])
    keep, send = split_bit(pieces, c, 1)
    keep = keep + swap(send.astype(BF16), "tp", 1).astype(F32)
    keep, send = split_bit(keep, y, 0)
    piece = (keep + swap(send.astype(BF16), "tp", 2).astype(F32))[0, 0].astype(BF16)
    groups = jnp.stack([piece] + [swap(piece, "ctx", k) for k in range(1, GROUP)])
    mine = [pick(groups, (t ^ z) ^ k) for k in range(GROUP)]
    mine = jnp.stack([mine[0]] + [swap(mine[k], "tp", k) for k in range(1, GROUP)])
    shard_qkv = jnp.concatenate([pick(mine, t ^ k) for k in range(GROUP)], 0).astype(F32)

    sums = jnp.stack(
        [
            jnp.sum(d_first * normal_a, 0),
            jnp.sum(d_first, 0),
            jnp.sum(own_cot * normal_f, 0),
            jnp.sum(own_cot, 0),
        ]
    )
    sums = turn(sums)
    sums = sums + swap(sums, "tp", 1)
    sums = sums + swap(sums, "tp", 2)
    sums = sums + swap(sums, "ctx", 1)
    sums = sums + swap(sums, "ctx", 2)
    sums = sums + swap(sums, "dp", 1, 2) if pair else lax.psum(sums, "dp")

    return (
        outputs,
        input_grad,
        shard_qkv[:, :head_cols],
        shard_qkv[:, head_cols : 2 * head_cols],
        shard_qkv[:, 2 * head_cols :],
        shard_out,
        shard_in,
        shard_up,
        sums[0],
        sums[1],
        sums[2],
        sums[3],
    )


def solution(mesh):
    tokens = P("dp", "ctx", None)
    return jax.shard_map(
        functools.partial(per_device, mesh.shape["dp"]),
        mesh=mesh,
        in_specs=(
            tokens,
            P("dp", None),
            P("dp", "tp"),
            P("dp", "tp"),
            P("dp", "tp"),
            P("tp", "dp"),
            P("dp", "tp"),
            P("tp", "dp"),
            P(),
            P(),
            P(),
            P(),
            tokens,
        ),
        out_specs=(
            tokens,
            tokens,
            P("dp", "tp"),
            P("dp", "tp"),
            P("dp", "tp"),
            P("tp", "dp"),
            P("dp", "tp"),
            P("tp", "dp"),
            P(),
            P(),
            P(),
            P(),
        ),
        check_vma=False,
    )
```

```python
import functools
import math

import jax
import jax.numpy as jnp
from jax import lax
from jax.experimental import pallas as pl
from jax.experimental.pallas import tpu as pltpu
from jax.sharding import PartitionSpec as P

HEAD_DIM = 64
HALF = HEAD_DIM // 2
DOCS = 16
EPSILON = 1e-06
MASKED = -1e30
LOG2E = 1.0 / math.log(2.0)
F32 = jnp.float32
BF16 = jnp.bfloat16
GROUP = 4
KEY_BLOCKS = 8


def dot(left, right, left_dim, right_dim):
    return lax.dot_general(
        left, right, (((left_dim,), (right_dim,)), ((), ())), preferred_element_type=F32
    )


def swap(value, axis, k, size=GROUP):
    return lax.ppermute(value, axis, [(i, i ^ k) for i in range(size)])


def after(value, *others):
    return lax.optimization_barrier((value,) + others)[0]


def pick(stack, index):
    return lax.dynamic_index_in_dim(stack, index, 0, keepdims=False)


def split_bit(value, bit, axis=0):
    half = value.shape[axis] // 2
    keep = lax.dynamic_slice_in_dim(value, bit * half, half, axis)
    send = lax.dynamic_slice_in_dim(value, (1 - bit) * half, half, axis)
    return keep, send


def join_bit(own, other, bit, axis=0):
    low = jnp.where(bit == 0, own, other)
    high = jnp.where(bit == 0, other, own)
    return jnp.concatenate([low, high], axis)


def block_mask(base, span_ref, shape):
    key_index = base + lax.broadcasted_iota(jnp.int32, shape, 0)
    return (key_index >= span_ref[0, 0:1, :]) & (key_index < span_ref[0, 1:2, :])


def ones_below(value):
    return jnp.concatenate([value, jnp.ones((16, value.shape[1]), BF16)])


def minus_below(value, row):
    high = row.astype(BF16)
    rest = row - high.astype(F32)
    mid = rest.astype(BF16)
    last = (rest - mid.astype(F32)).astype(BF16)
    index = lax.broadcasted_iota(jnp.int32, (16, value.shape[1]), 0)
    parts = jnp.where(
        index == 0,
        high.astype(F32),
        jnp.where(index == 1, mid.astype(F32), jnp.where(index == 2, last.astype(F32), 0.0)),
    )
    return jnp.concatenate([value, (-parts).astype(BF16)])


def pair_flag(a, b):
    return jnp.where(a + b == 0, 0, jnp.where(a + b == 4, 2, 1))


def each_block(flags, i, work):
    def step(j, carry):
        flag = pair_flag(flags[i * KEY_BLOCKS + j], flags[i * KEY_BLOCKS + j + KEY_BLOCKS // 2])

        @pl.when(flag == 1)
        def _():
            work(j, True)

        @pl.when(flag == 2)
        def _():
            work(j, False)

        return carry

    lax.fori_loop(0, KEY_BLOCKS // 2, step, 0)


def attend_kernel(
    first, flags, bases, q_ref, k_ref, v_ref, span_ref, o_ref, lse_ref, m_s, q_s, acc_s
):
    i = first + pl.program_id(0)
    heads = q_ref.shape[1] // HEAD_DIM
    rows = q_ref.shape[2]
    parts = [slice(h * HEAD_DIM, (h + 1) * HEAD_DIM) for h in range(heads)]
    m_s[...] = jnp.full(m_s.shape, MASKED, F32)
    acc_s[...] = jnp.zeros(acc_s.shape, F32)

    def find_max(j, masked):
        both = (j, j + KEY_BLOCKS // 2)
        scores = [
            [dot(k_ref[b, part, :], q_ref[0, part, :], 0, 0) for part in parts] for b in both
        ]
        if masked:
            for n, b in enumerate(both):
                ok = block_mask(bases[b], span_ref, (rows, rows))
                scores[n] = [jnp.where(ok, s, MASKED) for s in scores[n]]
        tops = [
            [jnp.max(s.reshape(rows // 8, 8, rows), axis=0) for s in one] for one in scores
        ]
        for h in range(heads):
            m_s[h] = jnp.maximum(m_s[h], jnp.maximum(tops[0][h], tops[1][h]))

    each_block(flags, i, find_max)
    for h, part in enumerate(parts):
        top = jnp.max(m_s[h], axis=0, keepdims=True)
        lse_ref[0, h : h + 1, :] = top
        q_s[h] = minus_below(q_ref[0, part, :], top)

    def mix(j, masked):
        mixed = []
        for b in (j, j + KEY_BLOCKS // 2):
            probs = [
                jnp.exp2(dot(ones_below(k_ref[b, part, :]), q_s[h], 0, 0))
                for h, part in enumerate(parts)
            ]
            if masked:
                ok = block_mask(bases[b], span_ref, (rows, rows))
                probs = [jnp.where(ok, p, 0.0) for p in probs]
            mixed.append([
                dot(ones_below(v_ref[b, part, :]), p.astype(BF16), 1, 0)
                for part, p in zip(parts, probs)
            ])
        for h in range(heads):
            acc_s[h] += mixed[0][h] + mixed[1][h]

    each_block(flags, i, mix)
    for h, part in enumerate(parts):
        total = acc_s[h, HEAD_DIM : HEAD_DIM + 1, :]
        o_ref[0, part, :] = (acc_s[h, :HEAD_DIM, :] / total).astype(BF16)
        lse_ref[0, h : h + 1, :] = lse_ref[0, h : h + 1, :] + jnp.log2(total)


def attend(flags, bases, q, k, v, span, first, blocks):
    width, rows = q.shape[1:]
    heads = width // HEAD_DIM
    one = lambda shape: pl.BlockSpec((1,) + shape, lambda i, *_: (first + i, 0, 0))
    out = lambda shape: pl.BlockSpec((1,) + shape, lambda i, *_: (i, 0, 0))
    whole = pl.BlockSpec(k.shape, lambda i, *_: (0, 0, 0))
    return pl.pallas_call(
        functools.partial(attend_kernel, first),
        grid_spec=pltpu.PrefetchScalarGridSpec(
            num_scalar_prefetch=2,
            grid=(blocks,),
            in_specs=[one((width, rows)), whole, whole, one((2, rows))],
            out_specs=[out((width, rows)), out((heads, rows))],
            scratch_shapes=[
                pltpu.VMEM((heads, 8, rows), F32),
                pltpu.VMEM((heads, HEAD_DIM + 16, rows), BF16),
                pltpu.VMEM((heads, HEAD_DIM + 16, rows), F32),
            ],
        ),
        out_shape=[
            jax.ShapeDtypeStruct((blocks, width, rows), BF16),
            jax.ShapeDtypeStruct((blocks, heads, rows), F32),
        ],
        name="attend",
    )(flags, bases, q, k, v, span)


def attend_back_kernel(
    first, flags, bases, q_ref, k_ref, v_ref, span_ref, o_ref, d_ref, lse_ref, *refs
):
    if first == 0:
        dq_ref, dk_s, dv_s, q_s, d_s = refs
    else:
        dk_in, dv_in, dq_ref, own_k_ref, own_v_ref, far_k_ref, far_v_ref = refs[:7]
        dk_s, dv_s, q_s, d_s = refs[7:]
    i = first + pl.program_id(0)
    heads = q_ref.shape[1] // HEAD_DIM
    parts = [slice(h * HEAD_DIM, (h + 1) * HEAD_DIM) for h in range(heads)]
    rows = q_ref.shape[2]

    @pl.when(pl.program_id(0) == 0)
    def _():
        dk_s[...] = jnp.zeros(dk_s.shape, F32) if first == 0 else dk_in[...]
        dv_s[...] = jnp.zeros(dv_s.shape, F32) if first == 0 else dv_in[...]

    dq_ref[...] = jnp.zeros(dq_ref.shape, F32)
    for h, part in enumerate(parts):
        grad = d_ref[0, part, :]
        delta = jnp.sum(o_ref[0, part, :].astype(F32) * grad.astype(F32), axis=0, keepdims=True)
        q_s[h] = minus_below(q_ref[0, part, :], lse_ref[0, h : h + 1, :])
        d_s[h] = minus_below(grad, delta)

    def work(j, masked):
        results = []
        for b in (j, j + KEY_BLOCKS // 2):
            keys = [k_ref[b, part, :] for part in parts]
            probs = [jnp.exp2(dot(ones_below(keys[h]), q_s[h], 0, 0)) for h in range(heads)]
            if masked:
                ok = block_mask(bases[b], span_ref, (rows, rows))
                probs = [jnp.where(ok, p, 0.0) for p in probs]
            shifted = [
                dot(ones_below(v_ref[b, part, :]), d_s[h], 0, 0) for h, part in enumerate(parts)
            ]
            scores = [(p * s).astype(BF16) for p, s in zip(probs, shifted)]
            d_v = [dot(d_ref[0, part, :], p.astype(BF16), 1, 1) for part, p in zip(parts, probs)]
            d_k = [dot(q_ref[0, part, :], s, 1, 1) for part, s in zip(parts, scores)]
            d_q = [dot(k, s, 1, 0) for k, s in zip(keys, scores)]
            results.append((d_v, d_k, d_q))
        for n, b in enumerate((j, j + KEY_BLOCKS // 2)):
            d_v, d_k, d_q = results[n]
            for h, part in enumerate(parts):
                dv_s[b, part, :] += d_v[h]
                dk_s[b, part, :] += d_k[h]
        for h, part in enumerate(parts):
            dq_ref[0, part, :] += results[0][2][h] + results[1][2][h]

    each_block(flags, i, work)
    if first == 0:
        return

    @pl.when(pl.program_id(0) == pl.num_programs(0) - 1)
    def _():
        own = own_k_ref.shape[0]
        own_k_ref[...] = dk_s[:own]
        own_v_ref[...] = dv_s[:own]
        far_k_ref[...] = dk_s[own:].astype(BF16)
        far_v_ref[...] = dv_s[own:].astype(BF16)


def attend_back(flags, bases, q, k, v, span, o, grad, lse, first, sums):
    blocks = o.shape[0]
    width, rows = q.shape[1:]
    heads = width // HEAD_DIM
    at = lambda shape: pl.BlockSpec((1,) + shape, lambda i, *_: (first + i, 0, 0))
    one = lambda shape: pl.BlockSpec((1,) + shape, lambda i, *_: (i, 0, 0))
    whole = lambda n: pl.BlockSpec((n, width, rows), lambda i, *_: (0, 0, 0))
    total = jax.ShapeDtypeStruct(k.shape, F32)
    half = (k.shape[0] // 2, width, rows)
    out_shape = [jax.ShapeDtypeStruct((blocks, width, rows), F32)]
    out_specs = [one((width, rows))]
    scratch = [
        pltpu.VMEM((heads, HEAD_DIM + 16, rows), BF16),
        pltpu.VMEM((heads, HEAD_DIM + 16, rows), BF16),
    ]
    if first == 0:
        out_shape += [total, total]
        out_specs += [whole(k.shape[0])] * 2
    else:
        out_shape += [jax.ShapeDtypeStruct(half, d) for d in (F32, F32, BF16, BF16)]
        out_specs += [whole(half[0])] * 4
        scratch = [pltpu.VMEM(k.shape, F32), pltpu.VMEM(k.shape, F32)] + scratch
    return pl.pallas_call(
        functools.partial(attend_back_kernel, first),
        grid_spec=pltpu.PrefetchScalarGridSpec(
            num_scalar_prefetch=2,
            grid=(blocks,),
            in_specs=[at((width, rows)), whole(k.shape[0]), whole(k.shape[0]), at((2, rows))]
            + [one((width, rows)), one((width, rows)), one((heads, rows))]
            + [whole(k.shape[0])] * len(sums),
            out_specs=out_specs,
            scratch_shapes=scratch,
        ),
        out_shape=out_shape,
        name="attend_back",
    )(flags, bases, q, k, v, span, o, grad, lse, *sums)


def rotate(value, cosines, sines):
    rows = value.shape[-1]
    parts = value.reshape(-1, 2, HALF, rows)
    lead, trail = parts[:, 0], parts[:, 1]
    return jnp.stack(
        [lead * cosines - trail * sines, trail * cosines + lead * sines], axis=1
    ).reshape(value.shape)


def norm_stats(rows):
    centre = jnp.mean(rows, axis=-1, keepdims=True)
    centred = rows - centre
    spread = jnp.mean(centred * centred, axis=-1, keepdims=True)
    scale = lax.rsqrt(spread + EPSILON)
    return centred * scale, scale


def norm_back(grad, normal, scale, gain):
    dn = grad * gain
    return scale * (
        dn
        - jnp.mean(dn, axis=-1, keepdims=True)
        - normal * jnp.mean(dn * normal, axis=-1, keepdims=True)
    )


def per_device(
    dp_size, inputs, segment_ids, w_query, w_key, w_value, w_output, w_inner, w_outer,
    gain_attn, shift_attn, gain_ffn, shift_ffn, cotangent,
):
    seqs, local_rows, width = inputs.shape
    rows = local_rows // 2
    x = lax.axis_index("dp")
    z = lax.axis_index("ctx")
    t = lax.axis_index("tp")
    y, c = t // 2, t % 2
    pair = dp_size == 2
    head_cols = w_query.shape[1]
    half_width = width // 2
    group_cols = 3 * head_cols

    def turn(value):
        if not pair:
            return value
        own, other = split_bit(value, x, value.ndim - 1)
        return jnp.concatenate([own, other], value.ndim - 1)

    def corner(value):
        flat = lambda d, s: d * GROUP + s
        return lax.ppermute(
            value, ("dp", "tp"),
            [(flat(d, s), flat(d ^ 1, s ^ 2)) for d in range(2) for s in range(GROUP)],
        )

    def across(local):
        if not pair:
            return None, None
        return swap(local, "dp", 1, 2), swap(local, "tp", 2)

    def gather(local, across_x, across_y, far_corner, axis):
        if not pair:
            near = lax.all_gather(local, "dp", axis=axis, tiled=True)
            return near, swap(near, "tp", 2)
        return (
            jnp.concatenate([local, across_x], axis),
            jnp.concatenate([across_y, far_corner], axis),
        )

    def exchange(value, axis, k, size=GROUP):
        return swap(value.astype(BF16), axis, k, size).astype(F32)

    def sum_dp(value):
        if not pair:
            return lax.psum_scatter(
                value.astype(BF16), "dp", scatter_dimension=value.ndim - 1, tiled=True
            ).astype(F32)
        return value[..., :half_width] + exchange(value[..., half_width:], "dp", 1, 2)

    bit0, bit1 = z % 2, z // 2

    def ctx_first(value):
        keep, send = split_bit(value, bit0)
        return keep, swap(send.astype(BF16), "ctx", 1)

    def ctx_second(keep, got):
        keep, send = split_bit(keep + got.astype(F32), bit1)
        return (keep + exchange(send, "ctx", 2)).astype(BF16)

    def ctx_rest(keep):
        keep = join_bit(keep, swap(keep, "ctx", 2), bit1)
        return join_bit(keep, swap(keep, "ctx", 1), bit0).astype(F32)

    def own_tokens(value):
        return lax.dynamic_slice(value, (y, c * rows, 0), (1, rows, value.shape[2]))[0]

    own_in = turn(own_tokens(inputs))
    local = jnp.concatenate([w_query, w_key, w_value], 1)
    near, far = gather(local, *across(local), corner(local) if pair else None, 0)
    in_2 = swap(own_in, "ctx", 2)
    in_blocks = [own_in, swap(own_in, "ctx", 1), in_2, swap(in_2, "ctx", 1)]
    own_cot = turn(own_tokens(cotangent)).astype(F32)
    gain_a, shift_a, gain_f, shift_f = [
        turn(v)[None, :] for v in (gain_attn, shift_attn, gain_ffn, shift_ffn)
    ]
    def by_group(near, far):
        mine = jnp.stack([near, far])
        other = swap(mine, "tp", 1)
        stack = jnp.stack([mine[0], other[0], mine[1], other[1]])
        return [pick(stack, (t ^ z) ^ k) for k in range(GROUP)]

    w_qkv = by_group(near, far)
    mid = head_cols + w_outer.shape[0]
    down = jnp.concatenate([w_output, w_outer, w_inner.T])
    down = after(down, far)
    down_x, down_y = across(down)

    docs = pick(segment_ids, y)
    doc_names = jnp.arange(DOCS, dtype=jnp.int32)[:, None]
    doc_start = jnp.sum((docs[None, :] < doc_names).astype(jnp.int32), 1)
    doc_end = jnp.sum((docs[None, :] <= doc_names).astype(jnp.int32), 1)
    doc_blocks = docs.reshape(GROUP, 2, rows)
    order = jnp.stack([z ^ k for k in range(GROUP)])
    query_docs = jnp.stack([doc_blocks[z ^ k, c] for k in range(GROUP)])
    far_docs = jnp.stack([doc_blocks[z ^ k, 1 - c] for k in range(GROUP)])
    hot = query_docs[:, None, :] == doc_names[None]
    starts = jnp.sum(jnp.where(hot, doc_start[None, :, None], 0), 1)
    ends = jnp.sum(jnp.where(hot, doc_end[None, :, None], 0), 1)
    span = jnp.stack([starts, ends], 1)
    query_bases = (order * 2 + c) * rows
    bases = jnp.concatenate([query_bases, (order * 2 + 1 - c) * rows])
    key_docs = jnp.concatenate([query_docs, far_docs])
    key_low, key_high = key_docs[:, 0], key_docs[:, -1]
    low, high = query_docs[:, :1], query_docs[:, -1:]
    meets = (low <= key_high[None]) & (key_low[None] <= high)
    one_doc = (low == high) & (key_low == low) & (key_high == low)
    flags = jnp.where(meets, jnp.where(one_doc, 2, 1), 0).astype(jnp.int32).reshape(-1)
    position = (
        query_bases[:, None] + jnp.arange(rows, dtype=jnp.int32)[None] - starts
    ).astype(F32)
    theta = jnp.power(10000.0, -2.0 * jnp.arange(HALF, dtype=F32) / HEAD_DIM)
    angle = position[:, None, :] * theta[None, :, None]
    cosines, sines = jnp.cos(angle), jnp.sin(angle)

    factor = 1.0 / math.sqrt(HEAD_DIM)
    queries, keys, values = [], [], []
    for k, block in enumerate(in_blocks):
        lin = dot(w_qkv[0], block, 0, 1)
        query = rotate(lin[:head_cols], cosines[k], sines[k])
        queries.append((query * (factor * LOG2E)).astype(BF16))
        keys.append(rotate(lin[head_cols : 2 * head_cols], cosines[k], sines[k]).astype(BF16))
        values.append(lin[2 * head_cols :].astype(BF16))
    queries = jnp.stack(queries)
    own = jnp.stack(keys + values)
    got = swap(own, "tp", 1)
    down_corner = swap(after(down_x, own), "tp", 2) if pair else None
    keys = jnp.concatenate([own[:GROUP], got[:GROUP]])
    values = jnp.concatenate([own[GROUP:], got[GROUP:]])

    mixed_b, lse_b = attend(flags, bases, queries, keys, values, span, 2, 2)
    mixed_a, lse_a = attend(
        flags, after(bases, mixed_b), queries, keys, values, span, 0, 2
    )
    if pair:
        down_x, down_y, down_corner = [after(v, mixed_a) for v in (down_x, down_y, down_corner)]
    near, far = gather(down, down_x, down_y, down_corner, 1)
    w_out = by_group(near[:head_cols], far[:head_cols])
    w_up = jnp.concatenate([near[head_cols:mid], far[head_cols:mid]])
    w_in = jnp.concatenate([near[mid:], far[mid:]])
    own_mixed = [
        mixed_a[0], swap(mixed_a[1], "ctx", 1), swap(mixed_b[0], "ctx", 2), swap(mixed_b[1], "ctx", 3)
    ]
    attended = functools.reduce(
        jnp.add, [dot(own_mixed[k], w_out[k], 0, 0) for k in (3, 2, 0, 1)]
    )

    normal_a, scale_a = norm_stats(own_in.astype(F32) + attended)
    first = normal_a * gain_a + shift_a
    first_own = first.astype(BF16)
    first_low = jnp.concatenate([first_own, swap(first_own, "tp", 1)])
    inner = dot(first_low, w_in, 1, 1)
    below = 0.5 * (1.0 + lax.erf(inner * math.sqrt(0.5)))
    density = jnp.exp(-0.5 * inner * inner) * (1.0 / math.sqrt(2.0 * math.pi))
    active = (inner * below).astype(BF16)
    slope = (below + inner * density).astype(BF16)
    active, slope = lax.optimization_barrier((active, slope))
    feed = dot(active, w_up, 1, 0)
    feed = feed[:rows] + exchange(feed[rows:], "tp", 1)
    normal_f, scale_f = norm_stats(first + feed)
    second = (normal_f * gain_f + shift_f).astype(BF16)

    d_second = norm_back(own_cot, normal_f, scale_f, gain_f)
    d_feed_own = d_second.astype(BF16)
    d_feed = jnp.concatenate([d_feed_own, swap(d_feed_own, "tp", 1)])
    hidden_cut = active.shape[1] // 2
    up_cut, in_cut = hidden_cut // 2, hidden_cut * 2 // 3

    def pieces(left, right, cut):
        part = lambda lo, hi: dot(left[:, lo:hi], right, 0, 0)
        near_low, far_low = part(0, cut), part(hidden_cut, hidden_cut + cut)
        near_high = part(cut, hidden_cut)
        far_high = part(hidden_cut + cut, 2 * hidden_cut)
        return near_low, far_low, near_high, far_high

    def send_dp(high):
        return swap(high[:, half_width:].astype(BF16), "dp", 1, 2) if pair else None

    def keep_dp(high, got):
        if pair:
            return high[:, :half_width] + got.astype(F32)
        return sum_dp(high)

    up = pieces(active, d_feed, up_cut)
    up_high = jnp.concatenate([up[2], up[3]])
    up_got = (swap(up[1].astype(BF16), "tp", 2), send_dp(up_high))
    d_inner = (dot(d_feed, w_up, 1, 1) * slope).astype(BF16)
    hidden = dot(d_inner, w_in, 1, 0)
    d_first = d_second + hidden[:rows] + exchange(hidden[rows:], "tp", 1)
    d_resid = norm_back(d_first, normal_a, scale_a, gain_a)
    d_attended = d_resid.astype(BF16)

    sent = [dot(w_out[k], d_attended, 1, 1).astype(BF16) for k in range(GROUP)]
    sent = list(lax.optimization_barrier(tuple(sent)))
    d_mixed = [sent[0]] + [swap(sent[k], "ctx", k) for k in range(1, GROUP)]

    late_first = after(first_low, *sent)
    inside = pieces(d_inner, late_first, in_cut)
    late_resid = after(d_attended, *sent)
    grad_out = jnp.stack([dot(own_mixed[k], late_resid, 1, 0) for k in range(GROUP)])
    ordered = [pick(grad_out, (t ^ z) ^ k) for k in range(GROUP)]
    got = exchange(jnp.stack([ordered[1], ordered[3]]), "tp", 1)
    out_near, out_far = ordered[0] + got[0], ordered[2] + got[1]
    in_high = jnp.concatenate([inside[2], out_near, inside[3], out_far])
    in_got = (swap(inside[1].astype(BF16), "tp", 2), send_dp(in_high))

    def second_stage(near_low, high, got_low, got_high, *others):
        got_low = after(got_low, *others)
        low = near_low + got_low.astype(F32)
        high = keep_dp(high, after(got_high, *others) if pair else None)
        cut = high.shape[0] // 2
        high, far = high[:cut], high[cut:]
        return low, high, send_dp(low), swap(far.astype(BF16), "tp", 2)

    def last_stage(low, high, got_low, got_high, *others):
        low = keep_dp(low, after(got_low, *others) if pair else None)
        return jnp.concatenate([low, high + after(got_high, *others).astype(F32)])

    up_low, up_high, *up_got = second_stage(up[0], up_high, *up_got, *sent)
    dq_a, sum_k, sum_v = attend_back(
        flags, after(bases, up_low, up_high), queries, keys, values, span, mixed_a,
        jnp.stack(d_mixed[:2]), lse_a, 0, (),
    )
    up = last_stage(up_low, up_high, *up_got, dq_a)
    up_keep, up_got = ctx_first(up)
    in_low, in_high, *in_got = second_stage(inside[0], in_high, *in_got, dq_a)

    d_query, d_key, d_value, sent_key, sent_value = attend_back(
        flags, after(bases, up_keep, in_low, in_high), queries, keys, values, span,
        mixed_b, jnp.stack(d_mixed[2:]), lse_b, 2, (sum_k, sum_v),
    )
    mark = d_query
    d_query = [dq_a[0], dq_a[1], d_query[0], d_query[1]]
    sibling = exchange(jnp.stack([sent_key, sent_value]), "tp", 1)
    d_key = d_key + sibling[0]
    d_value = d_value + sibling[1]
    lin = [
        jnp.concatenate(
            [
                rotate(d_query[k] * factor, cosines[k], -sines[k]).astype(BF16),
                rotate(d_key[k] * (1.0 / LOG2E), cosines[k], -sines[k]).astype(BF16),
                d_value[k].astype(BF16),
            ]
        )
        for k in range(GROUP)
    ]
    received = [lin[0]] + [swap(lin[k], "ctx", k) for k in range(1, GROUP)]
    grad_qkv = functools.reduce(
        jnp.add, [dot(lin[k], in_blocks[k], 1, 0) for k in range(GROUP)]
    )
    through = functools.reduce(
        jnp.add, [dot(received[k], w_qkv[k], 0, 1) for k in range(GROUP)]
    )
    input_own = (d_resid + through).astype(BF16)

    def spread(value):
        value = turn(value)
        a = jnp.stack([value, swap(value, "tp", 2)])
        b = swap(a, "tp", 1)
        quad = [a[0], b[0], a[1], b[1]]
        quad = jnp.stack(quad)
        parts = [pick(quad, (k ^ t)) for k in range(GROUP)]
        return jnp.stack(parts).reshape(seqs, local_rows, width)

    outputs = spread(second)
    input_grad = spread(input_own)

    inside = last_stage(in_low, in_high, *in_got, mark)
    in_keep, in_got = ctx_first(after(inside, *lin))

    part = sum_dp(grad_qkv)
    both = ("ctx", "tp")
    up = ctx_second(up_keep, after(up_got, part))
    part = part + lax.ppermute(
        part.astype(BF16), both,
        [(g * 4 + s, g * 4 + (s ^ 2)) for g in range(4) for s in range(4) if s // 2 != g // 2],
    ).astype(F32)
    inside = ctx_second(in_keep, after(in_got, part))
    part = part + lax.ppermute(
        part.astype(BF16), both, [(g * 4 + (g ^ 1), g * 4 + g) for g in range(4)]
    ).astype(F32)
    shard_up = ctx_rest(after(up, part))
    shard_in = ctx_rest(inside)
    shard_out = shard_in[hidden_cut:]
    shard_in = shard_in[:hidden_cut]
    part = part.astype(BF16)
    moved = [
        lax.ppermute(part, both, [(g * 4 + g, (g ^ k) * 4 + g) for g in range(4)])
        for k in range(1, GROUP)
    ]
    shard_qkv = jnp.where(t == z, part, moved[0] + moved[1] + moved[2]).astype(F32)

    sums = jnp.stack(
        [
            jnp.sum(d_first * normal_a, 0),
            jnp.sum(d_first, 0),
            jnp.sum(own_cot * normal_f, 0),
            jnp.sum(own_cot, 0),
        ]
    )
    sums = after(turn(sums), *lin)
    sums = sums + swap(sums, "tp", 1)
    sums = sums + swap(sums, "tp", 2)
    sums = after(sums, input_own)
    sums = sums + swap(sums, "dp", 1, 2) if pair else lax.psum(sums, "dp")
    sums = sums + swap(sums, "ctx", 1)
    sums = sums + swap(sums, "ctx", 2)

    return (
        outputs,
        input_grad,
        shard_qkv[:head_cols].T,
        shard_qkv[head_cols : 2 * head_cols].T,
        shard_qkv[2 * head_cols :].T,
        shard_out,
        shard_in.T,
        shard_up,
        sums[0],
        sums[1],
        sums[2],
        sums[3],
    )


def solution(mesh):
    tokens = P("dp", "ctx", None)
    return jax.shard_map(
        functools.partial(per_device, mesh.shape["dp"]),
        mesh=mesh,
        in_specs=(
            tokens,
            P("dp", None),
            P("dp", "tp"),
            P("dp", "tp"),
            P("dp", "tp"),
            P("tp", "dp"),
            P("dp", "tp"),
            P("tp", "dp"),
            P(),
            P(),
            P(),
            P(),
            tokens,
        ),
        out_specs=(
            tokens,
            tokens,
            P("dp", "tp"),
            P("dp", "tp"),
            P("dp", "tp"),
            P("tp", "dp"),
            P("dp", "tp"),
            P("tp", "dp"),
            P(),
            P(),
            P(),
            P(),
        ),
        check_vma=False,
    )
```

```python
import functools
import math

import jax
import jax.numpy as jnp
from jax import lax
from jax.experimental import pallas as pl
from jax.experimental.pallas import tpu as pltpu
from jax.sharding import PartitionSpec as P

HEAD_DIM = 64
HALF = HEAD_DIM // 2
DOCS = 16
EPSILON = 1e-06
MASKED = -1e30
LOG2E = 1.0 / math.log(2.0)
F32 = jnp.float32
BF16 = jnp.bfloat16
GROUP = 4
KEY_BLOCKS = 8


def dot(left, right, left_dim, right_dim):
    return lax.dot_general(
        left, right, (((left_dim,), (right_dim,)), ((), ())), preferred_element_type=F32
    )


def swap(value, axis, k, size=GROUP):
    return lax.ppermute(value, axis, [(i, i ^ k) for i in range(size)])


def after(value, *others):
    return lax.optimization_barrier((value,) + others)[0]


def together(values, *others):
    there = [v for v in values if v is not None]
    there = iter(lax.optimization_barrier(tuple(there) + others)[: len(there)])
    return [None if v is None else next(there) for v in values]


def pick(stack, index):
    return lax.dynamic_index_in_dim(stack, index, 0, keepdims=False)


def split_bit(value, bit, axis=0):
    half = value.shape[axis] // 2
    keep = lax.dynamic_slice_in_dim(value, bit * half, half, axis)
    send = lax.dynamic_slice_in_dim(value, (1 - bit) * half, half, axis)
    return keep, send


def join_bit(own, other, bit, axis=0):
    low = jnp.where(bit == 0, own, other)
    high = jnp.where(bit == 0, other, own)
    return jnp.concatenate([low, high], axis)


def block_mask(base, span_ref, shape):
    key_index = base + lax.broadcasted_iota(jnp.int32, shape, 0)
    return (key_index >= span_ref[0, 0:1, :]) & (key_index < span_ref[0, 1:2, :])


def ones_below(value):
    return jnp.concatenate([value, jnp.ones((16, value.shape[1]), BF16)])


def minus_below(value, row):
    high = row.astype(BF16)
    rest = row - high.astype(F32)
    mid = rest.astype(BF16)
    last = (rest - mid.astype(F32)).astype(BF16)
    index = lax.broadcasted_iota(jnp.int32, (16, value.shape[1]), 0)
    parts = jnp.where(
        index == 0,
        high.astype(F32),
        jnp.where(index == 1, mid.astype(F32), jnp.where(index == 2, last.astype(F32), 0.0)),
    )
    return jnp.concatenate([value, (-parts).astype(BF16)])


def pair_flag(a, b):
    return jnp.where(a + b == 0, 0, jnp.where(a + b == 4, 2, 1))


def each_block(flags, i, work):
    def step(j, carry):
        flag = pair_flag(flags[i * KEY_BLOCKS + j], flags[i * KEY_BLOCKS + j + KEY_BLOCKS // 2])

        @pl.when(flag == 1)
        def _():
            work(j, True)

        @pl.when(flag == 2)
        def _():
            work(j, False)

        return carry

    lax.fori_loop(0, KEY_BLOCKS // 2, step, 0)


def attend_kernel(
    first, flags, bases, q_ref, k_ref, v_ref, span_ref, o_ref, lse_ref, m_s, q_s, acc_s
):
    i = first + pl.program_id(0)
    heads = q_ref.shape[1] // HEAD_DIM
    rows = q_ref.shape[2]
    parts = [slice(h * HEAD_DIM, (h + 1) * HEAD_DIM) for h in range(heads)]
    m_s[...] = jnp.full(m_s.shape, MASKED, F32)
    acc_s[...] = jnp.zeros(acc_s.shape, F32)

    def find_max(j, masked):
        both = (j, j + KEY_BLOCKS // 2)
        scores = [
            [dot(k_ref[b, part, :], q_ref[0, part, :], 0, 0) for part in parts] for b in both
        ]
        if masked:
            for n, b in enumerate(both):
                ok = block_mask(bases[b], span_ref, (rows, rows))
                scores[n] = [jnp.where(ok, s, MASKED) for s in scores[n]]
        tops = [
            [jnp.max(s.reshape(rows // 8, 8, rows), axis=0) for s in one] for one in scores
        ]
        for h in range(heads):
            m_s[h] = jnp.maximum(m_s[h], jnp.maximum(tops[0][h], tops[1][h]))

    each_block(flags, i, find_max)
    for h, part in enumerate(parts):
        top = jnp.max(m_s[h], axis=0, keepdims=True)
        lse_ref[0, h : h + 1, :] = top
        q_s[h] = minus_below(q_ref[0, part, :], top)

    def mix(j, masked):
        mixed = []
        for b in (j, j + KEY_BLOCKS // 2):
            probs = [
                jnp.exp2(dot(ones_below(k_ref[b, part, :]), q_s[h], 0, 0))
                for h, part in enumerate(parts)
            ]
            if masked:
                ok = block_mask(bases[b], span_ref, (rows, rows))
                probs = [jnp.where(ok, p, 0.0) for p in probs]
            mixed.append([
                dot(ones_below(v_ref[b, part, :]), p.astype(BF16), 1, 0)
                for part, p in zip(parts, probs)
            ])
        for h in range(heads):
            acc_s[h] += mixed[0][h] + mixed[1][h]

    each_block(flags, i, mix)
    for h, part in enumerate(parts):
        total = acc_s[h, HEAD_DIM : HEAD_DIM + 1, :]
        o_ref[0, part, :] = (acc_s[h, :HEAD_DIM, :] / total).astype(BF16)
        lse_ref[0, h : h + 1, :] = lse_ref[0, h : h + 1, :] + jnp.log2(total)


def attend(flags, bases, q, k, v, span, first, blocks):
    width, rows = q.shape[1:]
    heads = width // HEAD_DIM
    one = lambda shape: pl.BlockSpec((1,) + shape, lambda i, *_: (first + i, 0, 0))
    out = lambda shape: pl.BlockSpec((1,) + shape, lambda i, *_: (i, 0, 0))
    whole = pl.BlockSpec(k.shape, lambda i, *_: (0, 0, 0))
    return pl.pallas_call(
        functools.partial(attend_kernel, first),
        grid_spec=pltpu.PrefetchScalarGridSpec(
            num_scalar_prefetch=2,
            grid=(blocks,),
            in_specs=[one((width, rows)), whole, whole, one((2, rows))],
            out_specs=[out((width, rows)), out((heads, rows))],
            scratch_shapes=[
                pltpu.VMEM((heads, 8, rows), F32),
                pltpu.VMEM((heads, HEAD_DIM + 16, rows), BF16),
                pltpu.VMEM((heads, HEAD_DIM + 16, rows), F32),
            ],
        ),
        out_shape=[
            jax.ShapeDtypeStruct((blocks, width, rows), BF16),
            jax.ShapeDtypeStruct((blocks, heads, rows), F32),
        ],
        name="attend",
    )(flags, bases, q, k, v, span)


def attend_back_kernel(
    first, flags, bases, q_ref, k_ref, v_ref, span_ref, o_ref, d_ref, lse_ref, *refs
):
    if first:
        dq_ref, dk_s, dv_s, q_s, d_s = refs
    else:
        dk_in, dv_in, dq_ref, own_k_ref, own_v_ref, far_k_ref, far_v_ref = refs[:7]
        dk_s, dv_s, q_s, d_s = refs[7:]
    i = first + pl.program_id(0)
    heads = q_ref.shape[1] // HEAD_DIM
    parts = [slice(h * HEAD_DIM, (h + 1) * HEAD_DIM) for h in range(heads)]
    rows = q_ref.shape[2]

    @pl.when(pl.program_id(0) == 0)
    def _():
        dk_s[...] = jnp.zeros(dk_s.shape, F32) if first else dk_in[...]
        dv_s[...] = jnp.zeros(dv_s.shape, F32) if first else dv_in[...]

    dq_ref[...] = jnp.zeros(dq_ref.shape, F32)
    for h, part in enumerate(parts):
        grad = d_ref[0, part, :]
        delta = jnp.sum(o_ref[0, part, :].astype(F32) * grad.astype(F32), axis=0, keepdims=True)
        q_s[h] = minus_below(q_ref[0, part, :], lse_ref[0, h : h + 1, :])
        d_s[h] = minus_below(grad, delta)

    def work(j, masked):
        results = []
        for b in (j, j + KEY_BLOCKS // 2):
            keys = [k_ref[b, part, :] for part in parts]
            probs = [jnp.exp2(dot(ones_below(keys[h]), q_s[h], 0, 0)) for h in range(heads)]
            if masked:
                ok = block_mask(bases[b], span_ref, (rows, rows))
                probs = [jnp.where(ok, p, 0.0) for p in probs]
            shifted = [
                dot(ones_below(v_ref[b, part, :]), d_s[h], 0, 0) for h, part in enumerate(parts)
            ]
            scores = [(p * s).astype(BF16) for p, s in zip(probs, shifted)]
            d_v = [dot(d_ref[0, part, :], p.astype(BF16), 1, 1) for part, p in zip(parts, probs)]
            d_k = [dot(q_ref[0, part, :], s, 1, 1) for part, s in zip(parts, scores)]
            d_q = [dot(k, s, 1, 0) for k, s in zip(keys, scores)]
            results.append((d_v, d_k, d_q))
        for n, b in enumerate((j, j + KEY_BLOCKS // 2)):
            d_v, d_k, d_q = results[n]
            for h, part in enumerate(parts):
                dv_s[b, part, :] += d_v[h]
                dk_s[b, part, :] += d_k[h]
        for h, part in enumerate(parts):
            dq_ref[0, part, :] += results[0][2][h] + results[1][2][h]

    each_block(flags, i, work)
    if first:
        return

    @pl.when(pl.program_id(0) == pl.num_programs(0) - 1)
    def _():
        own = own_k_ref.shape[0]
        own_k_ref[...] = dk_s[:own]
        own_v_ref[...] = dv_s[:own]
        far_k_ref[...] = dk_s[own:].astype(BF16)
        far_v_ref[...] = dv_s[own:].astype(BF16)


def attend_back(flags, bases, q, k, v, span, o, grad, lse, first, sums):
    blocks = o.shape[0]
    width, rows = q.shape[1:]
    heads = width // HEAD_DIM
    at = lambda shape: pl.BlockSpec((1,) + shape, lambda i, *_: (first + i, 0, 0))
    one = lambda shape: pl.BlockSpec((1,) + shape, lambda i, *_: (i, 0, 0))
    whole = lambda n: pl.BlockSpec((n, width, rows), lambda i, *_: (0, 0, 0))
    total = jax.ShapeDtypeStruct(k.shape, F32)
    half = (k.shape[0] // 2, width, rows)
    out_shape = [jax.ShapeDtypeStruct((blocks, width, rows), F32)]
    out_specs = [one((width, rows))]
    scratch = [
        pltpu.VMEM((heads, HEAD_DIM + 16, rows), BF16),
        pltpu.VMEM((heads, HEAD_DIM + 16, rows), BF16),
    ]
    if first:
        out_shape += [total, total]
        out_specs += [whole(k.shape[0])] * 2
    else:
        out_shape += [jax.ShapeDtypeStruct(half, d) for d in (F32, F32, BF16, BF16)]
        out_specs += [whole(half[0])] * 4
        scratch = [pltpu.VMEM(k.shape, F32), pltpu.VMEM(k.shape, F32)] + scratch
    return pl.pallas_call(
        functools.partial(attend_back_kernel, first),
        grid_spec=pltpu.PrefetchScalarGridSpec(
            num_scalar_prefetch=2,
            grid=(blocks,),
            in_specs=[at((width, rows)), whole(k.shape[0]), whole(k.shape[0]), at((2, rows))]
            + [one((width, rows)), one((width, rows)), one((heads, rows))]
            + [whole(k.shape[0])] * len(sums),
            out_specs=out_specs,
            scratch_shapes=scratch,
        ),
        out_shape=out_shape,
        name="attend_back",
    )(flags, bases, q, k, v, span, o, grad, lse, *sums)


def rotate(value, cosines, sines):
    rows = value.shape[-1]
    parts = value.reshape(-1, 2, HALF, rows)
    lead, trail = parts[:, 0], parts[:, 1]
    return jnp.stack(
        [lead * cosines - trail * sines, trail * cosines + lead * sines], axis=1
    ).reshape(value.shape)


def norm_stats(rows):
    centre = jnp.mean(rows, axis=-1, keepdims=True)
    centred = rows - centre
    spread = jnp.mean(centred * centred, axis=-1, keepdims=True)
    scale = lax.rsqrt(spread + EPSILON)
    return centred * scale, scale


def norm_back(grad, normal, scale, gain):
    dn = grad * gain
    return scale * (
        dn
        - jnp.mean(dn, axis=-1, keepdims=True)
        - normal * jnp.mean(dn * normal, axis=-1, keepdims=True)
    )


def per_device(
    dp_size, inputs, segment_ids, w_query, w_key, w_value, w_output, w_inner, w_outer,
    gain_attn, shift_attn, gain_ffn, shift_ffn, cotangent,
):
    seqs, local_rows, width = inputs.shape
    rows = local_rows // 2
    x = lax.axis_index("dp")
    z = lax.axis_index("ctx")
    t = lax.axis_index("tp")
    y, c = t // 2, t % 2
    pair = dp_size == 2
    head_cols = w_query.shape[1]
    half_width = width // 2
    group_cols = 3 * head_cols

    def turn(value):
        if not pair:
            return value
        own, other = split_bit(value, x, value.ndim - 1)
        return jnp.concatenate([own, other], value.ndim - 1)

    def corner(value):
        flat = lambda d, s: d * GROUP + s
        return lax.ppermute(
            value, ("dp", "tp"),
            [(flat(d, s), flat(d ^ 1, s ^ 2)) for d in range(2) for s in range(GROUP)],
        )

    def across(local):
        if not pair:
            return None, None
        return swap(local, "dp", 1, 2), swap(local, "tp", 2)

    def gather(local, across_x, across_y, far_corner, axis):
        if not pair:
            near = lax.all_gather(local, "dp", axis=axis, tiled=True)
            return near, swap(near, "tp", 2)
        return (
            jnp.concatenate([local, across_x], axis),
            jnp.concatenate([across_y, far_corner], axis),
        )

    def exchange(value, axis, k, size=GROUP):
        return swap(value.astype(BF16), axis, k, size).astype(F32)

    def sum_dp(value):
        if not pair:
            return lax.psum_scatter(
                value.astype(BF16), "dp", scatter_dimension=value.ndim - 1, tiled=True
            ).astype(F32)
        return value[..., :half_width] + exchange(value[..., half_width:], "dp", 1, 2)

    bit0, bit1 = z % 2, z // 2

    def ctx_first(value):
        keep, send = split_bit(value, bit0)
        return keep, swap(send.astype(BF16), "ctx", 1)

    def ctx_second(keep, got):
        keep, send = split_bit(keep + got.astype(F32), bit1)
        return keep, swap(send.astype(BF16), "ctx", 2)

    def ctx_third(keep, got):
        keep = (keep + got.astype(F32)).astype(BF16)
        return join_bit(keep, swap(keep, "ctx", 2), bit1)

    def own_tokens(value):
        return lax.dynamic_slice(value, (y, c * rows, 0), (1, rows, value.shape[2]))[0]

    own_in = turn(own_tokens(inputs))
    local = jnp.concatenate([w_query, w_key, w_value], 1)
    near, far = gather(local, *across(local), corner(local) if pair else None, 0)
    in_2 = swap(own_in, "ctx", 2)
    in_blocks = [own_in, swap(own_in, "ctx", 1), in_2, swap(in_2, "ctx", 1)]
    own_cot = turn(own_tokens(cotangent)).astype(F32)
    gain_a, shift_a, gain_f, shift_f = [
        turn(v)[None, :] for v in (gain_attn, shift_attn, gain_ffn, shift_ffn)
    ]
    def by_group(near, far):
        mine = jnp.stack([near, far])
        other = swap(mine, "tp", 1)
        stack = jnp.stack([mine[0], other[0], mine[1], other[1]])
        return [pick(stack, (t ^ z) ^ k) for k in range(GROUP)]

    w_qkv = by_group(near, far)
    mid = head_cols + w_outer.shape[0]
    down = jnp.concatenate([w_output, w_outer, w_inner.T])
    down = after(down, far)
    down_x, down_y = across(down)

    docs = pick(segment_ids, y)
    doc_names = jnp.arange(DOCS, dtype=jnp.int32)[:, None]
    doc_start = jnp.sum((docs[None, :] < doc_names).astype(jnp.int32), 1)
    doc_end = jnp.sum((docs[None, :] <= doc_names).astype(jnp.int32), 1)
    doc_blocks = docs.reshape(GROUP, 2, rows)
    order = jnp.stack([z ^ k for k in range(GROUP)])
    query_docs = jnp.stack([doc_blocks[z ^ k, c] for k in range(GROUP)])
    far_docs = jnp.stack([doc_blocks[z ^ k, 1 - c] for k in range(GROUP)])
    hot = query_docs[:, None, :] == doc_names[None]
    starts = jnp.sum(jnp.where(hot, doc_start[None, :, None], 0), 1)
    ends = jnp.sum(jnp.where(hot, doc_end[None, :, None], 0), 1)
    span = jnp.stack([starts, ends], 1)
    query_bases = (order * 2 + c) * rows
    bases = jnp.concatenate([query_bases, (order * 2 + 1 - c) * rows])
    key_docs = jnp.concatenate([query_docs, far_docs])
    key_low, key_high = key_docs[:, 0], key_docs[:, -1]
    low, high = query_docs[:, :1], query_docs[:, -1:]
    meets = (low <= key_high[None]) & (key_low[None] <= high)
    one_doc = (low == high) & (key_low == low) & (key_high == low)
    flags = jnp.where(meets, jnp.where(one_doc, 2, 1), 0).astype(jnp.int32).reshape(-1)
    position = (
        query_bases[:, None] + jnp.arange(rows, dtype=jnp.int32)[None] - starts
    ).astype(F32)
    theta = jnp.power(10000.0, -2.0 * jnp.arange(HALF, dtype=F32) / HEAD_DIM)
    angle = position[:, None, :] * theta[None, :, None]
    cosines, sines = jnp.cos(angle), jnp.sin(angle)

    factor = 1.0 / math.sqrt(HEAD_DIM)
    queries, keys, values = [], [], []
    for k, block in enumerate(in_blocks):
        lin = dot(w_qkv[0], block, 0, 1)
        query = rotate(lin[:head_cols], cosines[k], sines[k])
        queries.append((query * (factor * LOG2E)).astype(BF16))
        keys.append(rotate(lin[head_cols : 2 * head_cols], cosines[k], sines[k]).astype(BF16))
        values.append(lin[2 * head_cols :].astype(BF16))
    queries = jnp.stack(queries)
    own = jnp.stack(keys + values)
    got = swap(own, "tp", 1)
    keys = jnp.concatenate([own[:GROUP], got[:GROUP]])
    values = jnp.concatenate([own[GROUP:], got[GROUP:]])

    mixed_b, lse_b = attend(flags, bases, queries, keys, values, span, 2, 2)
    landed = [down_x, down_y] if pair else []
    mixed_0, lse_0 = attend(
        flags, after(bases, mixed_b, *landed), queries, keys, values, span, 0, 1
    )
    down_corner = None
    if pair:
        cut = down.shape[0] // 2
        late_x, late_y = after(down_x, mixed_b), after(down_y, mixed_b)
        low, high = swap(late_x[:cut], "tp", 2), swap(late_y[cut:], "dp", 1, 2)
        landed = [low, high]
    got_b = [swap(mixed_b[k], "ctx", k + 2) for k in range(2)]
    mixed_1, lse_1 = attend(
        flags, after(bases, mixed_0, *got_b, *landed), queries, keys, values, span, 1, 1
    )
    mixed_a, lse_a = jnp.concatenate([mixed_0, mixed_1]), jnp.concatenate([lse_0, lse_1])
    if pair:
        down_corner = jnp.concatenate([after(low, mixed_1), after(high, mixed_1)])
        down_x, down_y = after(down_x, mixed_1), after(down_y, mixed_1)
    near, far = gather(down, down_x, down_y, down_corner, 1)
    w_out = by_group(near[:head_cols], far[:head_cols])
    w_up = jnp.concatenate([near[head_cols:mid], far[head_cols:mid]])
    w_in = jnp.concatenate([near[mid:], far[mid:]])
    own_mixed = [mixed_0[0], swap(mixed_1[0], "ctx", 1)] + [after(g, mixed_1) for g in got_b]
    attended = functools.reduce(
        jnp.add, [dot(own_mixed[k], w_out[k], 0, 0) for k in (3, 2, 0, 1)]
    )

    normal_a, scale_a = norm_stats(own_in.astype(F32) + attended)
    first = normal_a * gain_a + shift_a
    first_own = first.astype(BF16)
    first_low = jnp.concatenate([first_own, swap(first_own, "tp", 1)])
    inner = dot(first_low, w_in, 1, 1)
    below = 0.5 * (1.0 + lax.erf(inner * math.sqrt(0.5)))
    density = jnp.exp(-0.5 * inner * inner) * (1.0 / math.sqrt(2.0 * math.pi))
    active = (inner * below).astype(BF16)
    slope = (below + inner * density).astype(BF16)
    active, slope = lax.optimization_barrier((active, slope))
    feed = dot(active, w_up, 1, 0)
    feed = feed[:rows] + exchange(feed[rows:], "tp", 1)
    normal_f, scale_f = norm_stats(first + feed)
    second = (normal_f * gain_f + shift_f).astype(BF16)

    def spread(own, got):
        quad = jnp.stack([own[0], got[0], own[1], got[1]])
        parts = [pick(quad, (k ^ t)) for k in range(GROUP)]
        return jnp.stack(parts).reshape(seqs, local_rows, width)

    d_second = norm_back(own_cot, normal_f, scale_f, gain_f)
    d_feed_own = d_second.astype(BF16)
    d_feed = jnp.concatenate([d_feed_own, swap(d_feed_own, "tp", 1)])
    hidden_cut = active.shape[1] // 2
    up_cut, in_cut = hidden_cut // 2, hidden_cut * 2 // 3

    def pieces(left, right, cut):
        part = lambda lo, hi: dot(left[:, lo:hi], right, 0, 0)
        near_low, far_low = part(0, cut), part(hidden_cut, hidden_cut + cut)
        near_high = part(cut, hidden_cut)
        far_high = part(hidden_cut + cut, 2 * hidden_cut)
        return near_low, far_low, near_high, far_high

    def send_dp(high):
        return swap(high[:, half_width:].astype(BF16), "dp", 1, 2) if pair else None

    def keep_dp(high, got):
        if pair:
            return high[:, :half_width] + got.astype(F32)
        return sum_dp(high)

    up = pieces(active, d_feed, up_cut)
    up_high = jnp.concatenate([up[2], up[3]])
    up_got = (swap(up[1].astype(BF16), "tp", 2), send_dp(up_high))
    d_inner = (dot(d_feed, w_up, 1, 1) * slope).astype(BF16)
    hidden = dot(d_inner, w_in, 1, 0)
    d_first = d_second + hidden[:rows] + exchange(hidden[rows:], "tp", 1)
    d_resid = norm_back(d_first, normal_a, scale_a, gain_a)
    d_attended = d_resid.astype(BF16)

    sent = [dot(w_out[k], d_attended, 1, 1).astype(BF16) for k in range(GROUP)]
    sent = list(lax.optimization_barrier(tuple(sent)))
    d_mixed = [sent[0]] + [swap(sent[k], "ctx", k) for k in range(1, GROUP)]

    late_first = after(first_low, *sent)
    inside = pieces(d_inner, late_first, in_cut)
    late_resid = after(d_attended, *sent)
    grad_out = jnp.stack([dot(own_mixed[k], late_resid, 1, 0) for k in range(GROUP)])
    ordered = [pick(grad_out, (t ^ z) ^ k) for k in range(GROUP)]
    got = exchange(jnp.stack([ordered[1], ordered[3]]), "tp", 1)
    out_near, out_far = ordered[0] + got[0], ordered[2] + got[1]
    in_high = jnp.concatenate([inside[2], out_near, inside[3], out_far])
    in_got = (swap(inside[1].astype(BF16), "tp", 2), send_dp(in_high))

    def second_stage(near_low, high, got_low, got_high, *others):
        got_low = after(got_low, *others)
        low = near_low + got_low.astype(F32)
        high = keep_dp(high, after(got_high, *others) if pair else None)
        cut = high.shape[0] // 2
        high, far = high[:cut], high[cut:]
        return low, high, send_dp(low), swap(far.astype(BF16), "tp", 2)

    def last_stage(low, high, got_low, got_high, *others):
        if others:
            got_low, got_high = together([got_low, got_high], *others)
        low = keep_dp(low, got_low)
        return jnp.concatenate([low, high + got_high.astype(F32)])

    up_low, up_high, *up_got = second_stage(up[0], up_high, *up_got, *sent)
    dq_b, sum_k, sum_v = attend_back(
        flags, after(bases, up_low, up_high), queries, keys, values, span, mixed_b,
        jnp.stack(d_mixed[2:]), lse_b, 2, (),
    )
    turn_q = lambda v, k: rotate(v * factor, cosines[k], -sines[k]).astype(BF16)
    lin_q = [None, None, turn_q(dq_b[0], 2), turn_q(dq_b[1], 3)]
    got_q = [None, None, swap(lin_q[2], "ctx", 2), swap(lin_q[3], "ctx", 3)]
    own_out = turn(second)
    *up_got, far_out = together([*up_got, swap(own_out, "tp", 2)], dq_b)
    outs = jnp.stack([own_out, far_out])
    up = last_stage(up_low, up_high, *up_got)
    up_keep, up_got = ctx_first(up)
    in_low, in_high, *in_got = second_stage(inside[0], in_high, *in_got, dq_b)

    sums = jnp.stack(
        [
            jnp.sum(d_first * normal_a, 0),
            jnp.sum(d_first, 0),
            jnp.sum(own_cot * normal_f, 0),
            jnp.sum(own_cot, 0),
        ]
    )
    sums = turn(sums)
    sums = sums + after(swap(sums, "tp", 1), dq_b)
    dq_a, d_key, d_value, sent_key, sent_value = attend_back(
        flags, after(bases, up_keep, in_low, in_high, lin_q[2], lin_q[3]), queries, keys, values,
        span, mixed_a, jnp.stack(d_mixed[:2]), lse_a, 0, (sum_k, sum_v),
    )
    mark = dq_a
    lin_q[:2] = [turn_q(dq_a[0], 0), turn_q(dq_a[1], 1)]
    sums = sums + after(swap(sums, "tp", 2), mark)
    sibling = exchange(jnp.stack([sent_key, sent_value]), "tp", 1)
    got_q = [None, None] + together(got_q[2:], mark)
    up_got, got_outs = together([up_got, swap(outs, "tp", 1)], mark)
    up_keep, up_got = ctx_second(up_keep, up_got)
    inside = last_stage(in_low, in_high, *in_got, mark)
    d_key = d_key + sibling[0]
    d_value = d_value + sibling[1]
    lin_kv = [
        jnp.concatenate(
            [
                rotate(d_key[k] * (1.0 / LOG2E), cosines[k], -sines[k]).astype(BF16),
                d_value[k].astype(BF16),
            ]
        )
        for k in range(GROUP)
    ]
    lin = [jnp.concatenate([lin_q[k], lin_kv[k]]) for k in range(GROUP)]
    in_keep, in_got = ctx_first(after(inside, *lin))
    grad_qkv = functools.reduce(
        jnp.add, [dot(lin[k], in_blocks[k], 1, 0) for k in range(GROUP)]
    )
    part = sum_dp(grad_qkv)
    arrived = [swap(lin[1], "ctx", 1)] + [swap(lin_kv[k], "ctx", k) for k in (2, 3)]
    *arrived, up_got, in_got = together([*arrived, up_got, in_got], grad_qkv.astype(BF16))
    received = [(lin[0], None), (arrived[0], None), (got_q[2], arrived[1]), (got_q[3], arrived[2])]
    through = []
    for k, (one, two) in enumerate(received):
        through.append(dot(one, w_qkv[k][:, : one.shape[0]], 0, 1))
        if two is not None:
            through.append(dot(two, w_qkv[k][:, one.shape[0] :], 0, 1))
    through = functools.reduce(jnp.add, through)
    input_own = (d_resid + through).astype(BF16)

    in_grad = turn(input_own)
    in_grad = jnp.stack([in_grad, swap(in_grad, "tp", 2)])
    outputs = spread(outs, got_outs)
    input_grad = spread(in_grad, swap(in_grad, "tp", 1))

    both = ("ctx", "tp")
    keep, send = split_bit(part, c)
    part = keep + exchange(send, "tp", 1)
    in_keep, in_got = ctx_second(in_keep, in_got)
    up = ctx_third(up_keep, up_got)
    part = part + lax.ppermute(
        part.astype(BF16), both,
        [(g * 4 + s, g * 4 + (s ^ 2)) for g in range(4) for s in range(4) if s // 2 != g // 2],
    ).astype(F32)
    part = part.astype(BF16)
    moved = lax.ppermute(
        part, both,
        [(g * 4 + s, (g ^ 2) * 4 + s) for g in range(4) for s in range(4) if s // 2 == g // 2],
    )
    held = jnp.where(y == z // 2, part, moved)
    inside = ctx_third(in_keep, in_got)
    shard_up = join_bit(up, swap(up, "ctx", 1), bit0).astype(F32)
    moved = after(swap(held, "ctx", 1), outputs, input_grad, shard_up)
    shard_in = join_bit(inside, swap(inside, "ctx", 1), bit0).astype(F32)
    mine = jnp.where(c == bit0, held, moved)
    theirs = jnp.where(c == bit0, moved, held)
    shard_qkv = join_bit(mine, swap(theirs, "tp", 1), c).astype(F32)
    shard_out = shard_in[hidden_cut:]
    shard_in = shard_in[:hidden_cut]

    got = swap(sums, "dp", 1, 2) if pair else None
    sums = sums + after(got, *lin) if pair else lax.psum(sums, "dp")
    sums = sums + after(swap(sums, "ctx", 1), input_own)
    sums = sums + swap(sums, "ctx", 2)

    return (
        outputs,
        input_grad,
        shard_qkv[:head_cols].T,
        shard_qkv[head_cols : 2 * head_cols].T,
        shard_qkv[2 * head_cols :].T,
        shard_out,
        shard_in.T,
        shard_up,
        sums[0],
        sums[1],
        sums[2],
        sums[3],
    )


def solution(mesh):
    tokens = P("dp", "ctx", None)
    return jax.shard_map(
        functools.partial(per_device, mesh.shape["dp"]),
        mesh=mesh,
        in_specs=(
            tokens,
            P("dp", None),
            P("dp", "tp"),
            P("dp", "tp"),
            P("dp", "tp"),
            P("tp", "dp"),
            P("dp", "tp"),
            P("tp", "dp"),
            P(),
            P(),
            P(),
            P(),
            tokens,
        ),
        out_specs=(
            tokens,
            tokens,
            P("dp", "tp"),
            P("dp", "tp"),
            P("dp", "tp"),
            P("tp", "dp"),
            P("dp", "tp"),
            P("tp", "dp"),
            P(),
            P(),
            P(),
            P(),
        ),
        check_vma=False,
    )
```

```python
import functools
import math

import jax
import jax.numpy as jnp
from jax import lax
from jax.experimental import pallas as pl
from jax.experimental.pallas import tpu as pltpu
from jax.sharding import PartitionSpec as P

HEAD_DIM = 64
HALF = HEAD_DIM // 2
DOCS = 16
EPSILON = 1e-06
MASKED = -1e30
LOG2E = 1.0 / math.log(2.0)
F32 = jnp.float32
BF16 = jnp.bfloat16
GROUP = 4
KEY_BLOCKS = 8


def dot(left, right, left_dim, right_dim):
    return lax.dot_general(
        left, right, (((left_dim,), (right_dim,)), ((), ())), preferred_element_type=F32
    )


def swap(value, axis, k, size=GROUP):
    return lax.ppermute(value, axis, [(i, i ^ k) for i in range(size)])


def after(value, *others):
    return lax.optimization_barrier((value,) + others)[0]


def together(values, *others):
    there = [v for v in values if v is not None]
    there = iter(lax.optimization_barrier(tuple(there) + others)[: len(there)])
    return [None if v is None else next(there) for v in values]


def pick(stack, index):
    return lax.dynamic_index_in_dim(stack, index, 0, keepdims=False)


def split_bit(value, bit, axis=0):
    half = value.shape[axis] // 2
    keep = lax.dynamic_slice_in_dim(value, bit * half, half, axis)
    send = lax.dynamic_slice_in_dim(value, (1 - bit) * half, half, axis)
    return keep, send


def join_bit(own, other, bit, axis=0):
    low = jnp.where(bit == 0, own, other)
    high = jnp.where(bit == 0, other, own)
    return jnp.concatenate([low, high], axis)


def block_mask(base, span_ref, shape):
    key_index = base + lax.broadcasted_iota(jnp.int32, shape, 0)
    return (key_index >= span_ref[0, 0:1, :]) & (key_index < span_ref[0, 1:2, :])


def ones_below(value):
    return jnp.concatenate([value, jnp.ones((16, value.shape[1]), BF16)])


def minus_below(value, row):
    high = row.astype(BF16)
    rest = row - high.astype(F32)
    mid = rest.astype(BF16)
    last = (rest - mid.astype(F32)).astype(BF16)
    index = lax.broadcasted_iota(jnp.int32, (16, value.shape[1]), 0)
    parts = jnp.where(
        index == 0,
        high.astype(F32),
        jnp.where(index == 1, mid.astype(F32), jnp.where(index == 2, last.astype(F32), 0.0)),
    )
    return jnp.concatenate([value, (-parts).astype(BF16)])


def pair_flag(a, b):
    return jnp.where(a + b == 0, 0, jnp.where(a + b == 4, 2, 1))


def each_block(flags, i, work):
    def step(j, carry):
        flag = pair_flag(flags[i * KEY_BLOCKS + j], flags[i * KEY_BLOCKS + j + KEY_BLOCKS // 2])

        @pl.when(flag == 1)
        def _():
            work(j, True)

        @pl.when(flag == 2)
        def _():
            work(j, False)

        return carry

    lax.fori_loop(0, KEY_BLOCKS // 2, step, 0)


def attend_kernel(
    first, flags, bases, q_ref, k_ref, v_ref, span_ref, o_ref, lse_ref, m_s, q_s, acc_s
):
    i = first + pl.program_id(0)
    heads = q_ref.shape[1] // HEAD_DIM
    rows = q_ref.shape[2]
    parts = [slice(h * HEAD_DIM, (h + 1) * HEAD_DIM) for h in range(heads)]
    m_s[...] = jnp.full(m_s.shape, MASKED, F32)
    acc_s[...] = jnp.zeros(acc_s.shape, F32)

    def find_max(j, masked):
        both = (j, j + KEY_BLOCKS // 2)
        scores = [
            [dot(k_ref[b, part, :], q_ref[0, part, :], 0, 0) for part in parts] for b in both
        ]
        if masked:
            for n, b in enumerate(both):
                ok = block_mask(bases[b], span_ref, (rows, rows))
                scores[n] = [jnp.where(ok, s, MASKED) for s in scores[n]]
        tops = [
            [jnp.max(s.reshape(rows // 8, 8, rows), axis=0) for s in one] for one in scores
        ]
        for h in range(heads):
            m_s[h] = jnp.maximum(m_s[h], jnp.maximum(tops[0][h], tops[1][h]))

    each_block(flags, i, find_max)
    for h, part in enumerate(parts):
        top = jnp.max(m_s[h], axis=0, keepdims=True)
        lse_ref[0, h : h + 1, :] = top
        q_s[h] = minus_below(q_ref[0, part, :], top)

    def mix(j, masked):
        mixed = []
        for b in (j, j + KEY_BLOCKS // 2):
            probs = [
                jnp.exp2(dot(ones_below(k_ref[b, part, :]), q_s[h], 0, 0))
                for h, part in enumerate(parts)
            ]
            if masked:
                ok = block_mask(bases[b], span_ref, (rows, rows))
                probs = [jnp.where(ok, p, 0.0) for p in probs]
            mixed.append([
                dot(ones_below(v_ref[b, part, :]), p.astype(BF16), 1, 0)
                for part, p in zip(parts, probs)
            ])
        for h in range(heads):
            acc_s[h] += mixed[0][h] + mixed[1][h]

    each_block(flags, i, mix)
    for h, part in enumerate(parts):
        total = acc_s[h, HEAD_DIM : HEAD_DIM + 1, :]
        o_ref[0, part, :] = (acc_s[h, :HEAD_DIM, :] / total).astype(BF16)
        lse_ref[0, h : h + 1, :] = lse_ref[0, h : h + 1, :] + jnp.log2(total)


def attend(flags, bases, q, k, v, span, first, blocks):
    width, rows = q.shape[1:]
    heads = width // HEAD_DIM
    one = lambda shape: pl.BlockSpec((1,) + shape, lambda i, *_: (first + i, 0, 0))
    out = lambda shape: pl.BlockSpec((1,) + shape, lambda i, *_: (i, 0, 0))
    whole = pl.BlockSpec(k.shape, lambda i, *_: (0, 0, 0))
    return pl.pallas_call(
        functools.partial(attend_kernel, first),
        grid_spec=pltpu.PrefetchScalarGridSpec(
            num_scalar_prefetch=2,
            grid=(blocks,),
            in_specs=[one((width, rows)), whole, whole, one((2, rows))],
            out_specs=[out((width, rows)), out((heads, rows))],
            scratch_shapes=[
                pltpu.VMEM((heads, 8, rows), F32),
                pltpu.VMEM((heads, HEAD_DIM + 16, rows), BF16),
                pltpu.VMEM((heads, HEAD_DIM + 16, rows), F32),
            ],
        ),
        out_shape=[
            jax.ShapeDtypeStruct((blocks, width, rows), BF16),
            jax.ShapeDtypeStruct((blocks, heads, rows), F32),
        ],
        name="attend",
    )(flags, bases, q, k, v, span)


def attend_back_kernel(
    first, flags, bases, q_ref, k_ref, v_ref, span_ref, o_ref, d_ref, lse_ref, *refs
):
    if first:
        dq_ref, dk_s, dv_s, q_s, d_s = refs
    else:
        dk_in, dv_in, dq_ref, own_k_ref, own_v_ref, far_k_ref, far_v_ref = refs[:7]
        dk_s, dv_s, q_s, d_s = refs[7:]
    i = first + pl.program_id(0)
    heads = q_ref.shape[1] // HEAD_DIM
    parts = [slice(h * HEAD_DIM, (h + 1) * HEAD_DIM) for h in range(heads)]
    rows = q_ref.shape[2]

    @pl.when(pl.program_id(0) == 0)
    def _():
        dk_s[...] = jnp.zeros(dk_s.shape, F32) if first else dk_in[...]
        dv_s[...] = jnp.zeros(dv_s.shape, F32) if first else dv_in[...]

    dq_ref[...] = jnp.zeros(dq_ref.shape, F32)
    for h, part in enumerate(parts):
        grad = d_ref[0, part, :]
        delta = jnp.sum(o_ref[0, part, :].astype(F32) * grad.astype(F32), axis=0, keepdims=True)
        q_s[h] = minus_below(q_ref[0, part, :], lse_ref[0, h : h + 1, :])
        d_s[h] = minus_below(grad, delta)

    def work(j, masked):
        results = []
        for b in (j, j + KEY_BLOCKS // 2):
            keys = [k_ref[b, part, :] for part in parts]
            probs = [jnp.exp2(dot(ones_below(keys[h]), q_s[h], 0, 0)) for h in range(heads)]
            if masked:
                ok = block_mask(bases[b], span_ref, (rows, rows))
                probs = [jnp.where(ok, p, 0.0) for p in probs]
            shifted = [
                dot(ones_below(v_ref[b, part, :]), d_s[h], 0, 0) for h, part in enumerate(parts)
            ]
            scores = [(p * s).astype(BF16) for p, s in zip(probs, shifted)]
            d_v = [dot(d_ref[0, part, :], p.astype(BF16), 1, 1) for part, p in zip(parts, probs)]
            d_k = [dot(q_ref[0, part, :], s, 1, 1) for part, s in zip(parts, scores)]
            d_q = [dot(k, s, 1, 0) for k, s in zip(keys, scores)]
            results.append((d_v, d_k, d_q))
        for n, b in enumerate((j, j + KEY_BLOCKS // 2)):
            d_v, d_k, d_q = results[n]
            for h, part in enumerate(parts):
                dv_s[b, part, :] += d_v[h]
                dk_s[b, part, :] += d_k[h]
        for h, part in enumerate(parts):
            dq_ref[0, part, :] += results[0][2][h] + results[1][2][h]

    each_block(flags, i, work)
    if first:
        return

    @pl.when(pl.program_id(0) == pl.num_programs(0) - 1)
    def _():
        own = own_k_ref.shape[0]
        own_k_ref[...] = dk_s[:own]
        own_v_ref[...] = dv_s[:own]
        far_k_ref[...] = dk_s[own:].astype(BF16)
        far_v_ref[...] = dv_s[own:].astype(BF16)


def attend_back(flags, bases, q, k, v, span, o, grad, lse, first, sums):
    blocks = o.shape[0]
    width, rows = q.shape[1:]
    heads = width // HEAD_DIM
    at = lambda shape: pl.BlockSpec((1,) + shape, lambda i, *_: (first + i, 0, 0))
    one = lambda shape: pl.BlockSpec((1,) + shape, lambda i, *_: (i, 0, 0))
    whole = lambda n: pl.BlockSpec((n, width, rows), lambda i, *_: (0, 0, 0))
    total = jax.ShapeDtypeStruct(k.shape, F32)
    half = (k.shape[0] // 2, width, rows)
    out_shape = [jax.ShapeDtypeStruct((blocks, width, rows), F32)]
    out_specs = [one((width, rows))]
    scratch = [
        pltpu.VMEM((heads, HEAD_DIM + 16, rows), BF16),
        pltpu.VMEM((heads, HEAD_DIM + 16, rows), BF16),
    ]
    if first:
        out_shape += [total, total]
        out_specs += [whole(k.shape[0])] * 2
    else:
        out_shape += [jax.ShapeDtypeStruct(half, d) for d in (F32, F32, BF16, BF16)]
        out_specs += [whole(half[0])] * 4
        scratch = [pltpu.VMEM(k.shape, F32), pltpu.VMEM(k.shape, F32)] + scratch
    return pl.pallas_call(
        functools.partial(attend_back_kernel, first),
        grid_spec=pltpu.PrefetchScalarGridSpec(
            num_scalar_prefetch=2,
            grid=(blocks,),
            in_specs=[at((width, rows)), whole(k.shape[0]), whole(k.shape[0]), at((2, rows))]
            + [one((width, rows)), one((width, rows)), one((heads, rows))]
            + [whole(k.shape[0])] * len(sums),
            out_specs=out_specs,
            scratch_shapes=scratch,
        ),
        out_shape=out_shape,
        name="attend_back",
    )(flags, bases, q, k, v, span, o, grad, lse, *sums)


def rotate(value, cosines, sines):
    rows = value.shape[-1]
    parts = value.reshape(-1, 2, HALF, rows)
    lead, trail = parts[:, 0], parts[:, 1]
    return jnp.stack(
        [lead * cosines - trail * sines, trail * cosines + lead * sines], axis=1
    ).reshape(value.shape)


def norm_stats(rows):
    centre = jnp.mean(rows, axis=-1, keepdims=True)
    centred = rows - centre
    spread = jnp.mean(centred * centred, axis=-1, keepdims=True)
    scale = lax.rsqrt(spread + EPSILON)
    return centred * scale, scale


def norm_back(grad, normal, scale, gain):
    dn = grad * gain
    return scale * (
        dn
        - jnp.mean(dn, axis=-1, keepdims=True)
        - normal * jnp.mean(dn * normal, axis=-1, keepdims=True)
    )


def per_device(
    dp_size, inputs, segment_ids, w_query, w_key, w_value, w_output, w_inner, w_outer,
    gain_attn, shift_attn, gain_ffn, shift_ffn, cotangent,
):
    seqs, local_rows, width = inputs.shape
    rows = local_rows // 2
    x = lax.axis_index("dp")
    z = lax.axis_index("ctx")
    t = lax.axis_index("tp")
    y, c = t // 2, t % 2
    pair = dp_size == 2
    head_cols = w_query.shape[1]
    half_width = width // 2
    group_cols = 3 * head_cols

    def turn(value):
        if not pair:
            return value
        own, other = split_bit(value, x, value.ndim - 1)
        return jnp.concatenate([own, other], value.ndim - 1)

    def corner(value):
        flat = lambda d, s: d * GROUP + s
        return lax.ppermute(
            value, ("dp", "tp"),
            [(flat(d, s), flat(d ^ 1, s ^ 2)) for d in range(2) for s in range(GROUP)],
        )

    def across(local):
        if not pair:
            return None, None
        return swap(local, "dp", 1, 2), swap(local, "tp", 2)

    def gather(local, across_x, across_y, far_corner, axis):
        if not pair:
            near = lax.all_gather(local, "dp", axis=axis, tiled=True)
            return near, swap(near, "tp", 2)
        return (
            jnp.concatenate([local, across_x], axis),
            jnp.concatenate([across_y, far_corner], axis),
        )

    def exchange(value, axis, k, size=GROUP):
        return swap(value.astype(BF16), axis, k, size).astype(F32)

    def sum_dp(value):
        if not pair:
            return lax.psum_scatter(
                value.astype(BF16), "dp", scatter_dimension=value.ndim - 1, tiled=True
            ).astype(F32)
        return value[..., :half_width] + exchange(value[..., half_width:], "dp", 1, 2)

    bit0, bit1 = z % 2, z // 2

    def ctx_first(value):
        keep, send = split_bit(value, bit0)
        return keep, swap(send.astype(BF16), "ctx", 1)

    def ctx_second(keep, got):
        keep, send = split_bit(keep + got.astype(F32), bit1)
        return keep, swap(send.astype(BF16), "ctx", 2)

    def ctx_third(keep, got):
        keep = (keep + got.astype(F32)).astype(BF16)
        return keep, swap(keep, "ctx", 2)

    def own_tokens(value):
        return lax.dynamic_slice(value, (y, c * rows, 0), (1, rows, value.shape[2]))[0]

    own_in = turn(own_tokens(inputs))
    local = jnp.concatenate([w_query, w_key, w_value], 1)
    near, far = gather(local, *across(local), corner(local) if pair else None, 0)
    in_2 = swap(own_in, "ctx", 2)
    in_blocks = [own_in, swap(own_in, "ctx", 1), in_2, swap(in_2, "ctx", 1)]
    own_cot = turn(own_tokens(cotangent)).astype(F32)
    gain_a, shift_a, gain_f, shift_f = [
        turn(v)[None, :] for v in (gain_attn, shift_attn, gain_ffn, shift_ffn)
    ]
    def by_group(near, far):
        mine = jnp.stack([near, far])
        other = swap(mine, "tp", 1)
        stack = jnp.stack([mine[0], other[0], mine[1], other[1]])
        return [pick(stack, (t ^ z) ^ k) for k in range(GROUP)]

    w_qkv = by_group(near, far)
    mid = head_cols + w_outer.shape[0]
    down = jnp.concatenate([w_output, w_outer, w_inner.T])
    down = after(down, far)
    down_x, down_y = across(down)

    docs = pick(segment_ids, y)
    doc_names = jnp.arange(DOCS, dtype=jnp.int32)[:, None]
    doc_start = jnp.sum((docs[None, :] < doc_names).astype(jnp.int32), 1)
    doc_end = jnp.sum((docs[None, :] <= doc_names).astype(jnp.int32), 1)
    doc_blocks = docs.reshape(GROUP, 2, rows)
    order = jnp.stack([z ^ k for k in range(GROUP)])
    query_docs = jnp.stack([doc_blocks[z ^ k, c] for k in range(GROUP)])
    far_docs = jnp.stack([doc_blocks[z ^ k, 1 - c] for k in range(GROUP)])
    hot = query_docs[:, None, :] == doc_names[None]
    starts = jnp.sum(jnp.where(hot, doc_start[None, :, None], 0), 1)
    ends = jnp.sum(jnp.where(hot, doc_end[None, :, None], 0), 1)
    span = jnp.stack([starts, ends], 1)
    query_bases = (order * 2 + c) * rows
    bases = jnp.concatenate([query_bases, (order * 2 + 1 - c) * rows])
    key_docs = jnp.concatenate([query_docs, far_docs])
    key_low, key_high = key_docs[:, 0], key_docs[:, -1]
    low, high = query_docs[:, :1], query_docs[:, -1:]
    meets = (low <= key_high[None]) & (key_low[None] <= high)
    one_doc = (low == high) & (key_low == low) & (key_high == low)
    flags = jnp.where(meets, jnp.where(one_doc, 2, 1), 0).astype(jnp.int32).reshape(-1)
    position = (
        query_bases[:, None] + jnp.arange(rows, dtype=jnp.int32)[None] - starts
    ).astype(F32)
    theta = jnp.power(10000.0, -2.0 * jnp.arange(HALF, dtype=F32) / HEAD_DIM)
    angle = position[:, None, :] * theta[None, :, None]
    cosines, sines = jnp.cos(angle), jnp.sin(angle)

    factor = 1.0 / math.sqrt(HEAD_DIM)
    queries, keys, values = [], [], []
    for k, block in enumerate(in_blocks):
        lin = dot(w_qkv[0], block, 0, 1)
        query = rotate(lin[:head_cols], cosines[k], sines[k])
        queries.append((query * (factor * LOG2E)).astype(BF16))
        keys.append(rotate(lin[head_cols : 2 * head_cols], cosines[k], sines[k]).astype(BF16))
        values.append(lin[2 * head_cols :].astype(BF16))
    queries = jnp.stack(queries)
    own = jnp.stack(keys + values)
    got = swap(own, "tp", 1)
    keys = jnp.concatenate([own[:GROUP], got[:GROUP]])
    values = jnp.concatenate([own[GROUP:], got[GROUP:]])

    mixed_b, lse_b = attend(flags, bases, queries, keys, values, span, 2, 2)
    landed = [down_x, down_y] if pair else []
    mixed_0, lse_0 = attend(
        flags, after(bases, mixed_b, *landed), queries, keys, values, span, 0, 1
    )
    down_corner = None
    if pair:
        cut = down.shape[0] // 2
        late_x, late_y = after(down_x, mixed_b), after(down_y, mixed_b)
        low, high = swap(late_x[:cut], "tp", 2), swap(late_y[cut:], "dp", 1, 2)
        landed = [low, high]
    got_b = [swap(mixed_b[k], "ctx", k + 2) for k in range(2)]
    mixed_1, lse_1 = attend(
        flags, after(bases, mixed_0, *got_b, *landed), queries, keys, values, span, 1, 1
    )
    mixed_a, lse_a = jnp.concatenate([mixed_0, mixed_1]), jnp.concatenate([lse_0, lse_1])
    if pair:
        down_corner = jnp.concatenate([after(low, mixed_1), after(high, mixed_1)])
        down_x, down_y = after(down_x, mixed_1), after(down_y, mixed_1)
    near, far = gather(down, down_x, down_y, down_corner, 1)
    w_out = by_group(near[:head_cols], far[:head_cols])
    w_up = jnp.concatenate([near[head_cols:mid], far[head_cols:mid]])
    w_in = jnp.concatenate([near[mid:], far[mid:]])
    own_mixed = [mixed_0[0], swap(mixed_1[0], "ctx", 1)] + [after(g, mixed_1) for g in got_b]
    attended = functools.reduce(
        jnp.add, [dot(own_mixed[k], w_out[k], 0, 0) for k in (3, 2, 0, 1)]
    )

    normal_a, scale_a = norm_stats(own_in.astype(F32) + attended)
    first = normal_a * gain_a + shift_a
    first_own = first.astype(BF16)
    first_low = jnp.concatenate([first_own, swap(first_own, "tp", 1)])
    inner = dot(first_low, w_in, 1, 1)
    below = 0.5 * (1.0 + lax.erf(inner * math.sqrt(0.5)))
    density = jnp.exp(-0.5 * inner * inner) * (1.0 / math.sqrt(2.0 * math.pi))
    active = (inner * below).astype(BF16)
    slope = (below + inner * density).astype(BF16)
    active, slope = lax.optimization_barrier((active, slope))
    feed = dot(active, w_up, 1, 0)
    feed = feed[:rows] + exchange(feed[rows:], "tp", 1)
    normal_f, scale_f = norm_stats(first + feed)
    second = (normal_f * gain_f + shift_f).astype(BF16)

    def spread(own, got):
        quad = jnp.stack([own[0], got[0], own[1], got[1]])
        parts = [pick(quad, (k ^ t)) for k in range(GROUP)]
        return jnp.stack(parts).reshape(seqs, local_rows, width)

    d_second = norm_back(own_cot, normal_f, scale_f, gain_f)
    d_feed_own = d_second.astype(BF16)
    d_feed = jnp.concatenate([d_feed_own, swap(d_feed_own, "tp", 1)])
    hidden_cut = active.shape[1] // 2
    up_cut, in_cut = hidden_cut // 2, hidden_cut * 2 // 3

    def pieces(left, right, cut):
        part = lambda lo, hi: dot(left[:, lo:hi], right, 0, 0)
        near_low, far_low = part(0, cut), part(hidden_cut, hidden_cut + cut)
        near_high = part(cut, hidden_cut)
        far_high = part(hidden_cut + cut, 2 * hidden_cut)
        return near_low, far_low, near_high, far_high

    def send_dp(high):
        return swap(high[:, half_width:].astype(BF16), "dp", 1, 2) if pair else None

    def keep_dp(high, got):
        if pair:
            return high[:, :half_width] + got.astype(F32)
        return sum_dp(high)

    up = pieces(active, d_feed, up_cut)
    up_high = jnp.concatenate([up[2], up[3]])
    up_got = (swap(up[1].astype(BF16), "tp", 2), send_dp(up_high))
    d_inner = (dot(d_feed, w_up, 1, 1) * slope).astype(BF16)
    hidden = dot(d_inner, w_in, 1, 0)
    d_first = d_second + hidden[:rows] + exchange(hidden[rows:], "tp", 1)
    d_resid = norm_back(d_first, normal_a, scale_a, gain_a)
    d_attended = d_resid.astype(BF16)

    sent = [dot(w_out[k], d_attended, 1, 1).astype(BF16) for k in range(GROUP)]
    sent = list(lax.optimization_barrier(tuple(sent)))
    d_mixed = [sent[0]] + [swap(sent[k], "ctx", k) for k in range(1, GROUP)]

    late_first = after(first_low, *sent)
    inside = pieces(d_inner, late_first, in_cut)
    late_resid = after(d_attended, *sent)
    grad_out = jnp.stack([dot(own_mixed[k], late_resid, 1, 0) for k in range(GROUP)])
    ordered = [pick(grad_out, (t ^ z) ^ k) for k in range(GROUP)]
    got = exchange(jnp.stack([ordered[1], ordered[3]]), "tp", 1)
    out_near, out_far = ordered[0] + got[0], ordered[2] + got[1]
    in_high = jnp.concatenate([inside[2], out_near, inside[3], out_far])
    in_got = (swap(inside[1].astype(BF16), "tp", 2), send_dp(in_high))

    def second_stage(near_low, high, got_low, got_high, *others):
        got_low = after(got_low, *others)
        low = near_low + got_low.astype(F32)
        high = keep_dp(high, after(got_high, *others) if pair else None)
        cut = high.shape[0] // 2
        high, far = high[:cut], high[cut:]
        return low, high, send_dp(low), swap(far.astype(BF16), "tp", 2)

    def last_stage(low, high, got_low, got_high, *others):
        if others:
            got_low, got_high = together([got_low, got_high], *others)
        low = keep_dp(low, got_low)
        return jnp.concatenate([low, high + got_high.astype(F32)])

    up_low, up_high, *up_got = second_stage(up[0], up_high, *up_got, *sent)
    dq_b, sum_k, sum_v = attend_back(
        flags, after(bases, up_low, up_high), queries, keys, values, span, mixed_b,
        jnp.stack(d_mixed[2:]), lse_b, 2, (),
    )
    turn_q = lambda v, k: rotate(v * factor, cosines[k], -sines[k]).astype(BF16)
    lin_q = [None, None, turn_q(dq_b[0], 2), turn_q(dq_b[1], 3)]
    got_q = [None, None, swap(lin_q[2], "ctx", 2), swap(lin_q[3], "ctx", 3)]
    own_out = turn(second)
    up_got = together(up_got, dq_b)
    up = last_stage(up_low, up_high, *up_got)
    up_keep, up_got = ctx_first(up)
    in_low, in_high, *in_got = second_stage(inside[0], in_high, *in_got, dq_b)

    sums = jnp.stack(
        [
            jnp.sum(d_first * normal_a, 0),
            jnp.sum(d_first, 0),
            jnp.sum(own_cot * normal_f, 0),
            jnp.sum(own_cot, 0),
        ]
    )
    sums = turn(sums)
    sums = sums + after(swap(sums, "tp", 1), dq_b)
    dq_a, d_key, d_value, sent_key, sent_value = attend_back(
        flags, after(bases, up_keep, in_low, in_high, lin_q[2], lin_q[3]), queries, keys, values,
        span, mixed_a, jnp.stack(d_mixed[:2]), lse_a, 0, (sum_k, sum_v),
    )
    mark = dq_a
    lin_q[:2] = [turn_q(dq_a[0], 0), turn_q(dq_a[1], 1)]
    sums = sums + after(swap(sums, "tp", 2), mark)
    sibling = exchange(jnp.stack([sent_key, sent_value]), "tp", 1)
    got_q = [None, None] + together(got_q[2:], mark)
    far_out = swap(after(own_out, mark, sent_key), "tp", 2)
    up_keep, up_got = ctx_second(up_keep, after(up_got, mark))
    inside = last_stage(in_low, in_high, *in_got, mark)
    d_key = d_key + sibling[0]
    d_value = d_value + sibling[1]
    lin_kv = [
        jnp.concatenate(
            [
                rotate(d_key[k] * (1.0 / LOG2E), cosines[k], -sines[k]).astype(BF16),
                d_value[k].astype(BF16),
            ]
        )
        for k in range(GROUP)
    ]
    lin = [jnp.concatenate([lin_q[k], lin_kv[k]]) for k in range(GROUP)]
    in_keep, in_got = ctx_first(after(inside, *lin))
    grad_qkv = functools.reduce(
        jnp.add, [dot(lin[k], in_blocks[k], 1, 0) for k in range(GROUP)]
    )
    part = sum_dp(grad_qkv)
    arrived = [swap(lin[1], "ctx", 1)] + [swap(lin_kv[k], "ctx", k) for k in (2, 3)]
    *arrived, up_got, in_got = together([*arrived, up_got, in_got], grad_qkv.astype(BF16))
    received = [(lin[0], None), (arrived[0], None), (got_q[2], arrived[1]), (got_q[3], arrived[2])]
    through = []
    for k, (one, two) in enumerate(received):
        through.append(dot(one, w_qkv[k][:, : one.shape[0]], 0, 1))
        if two is not None:
            through.append(dot(two, w_qkv[k][:, one.shape[0] :], 0, 1))
    through = functools.reduce(jnp.add, through)
    input_own = (d_resid + through).astype(BF16)

    in_grad = turn(input_own)
    in_grad = jnp.stack([in_grad, swap(in_grad, "tp", 2)])
    input_grad = spread(in_grad, swap(in_grad, "tp", 1))

    both = ("ctx", "tp")
    keep, send = split_bit(part, c)
    part = keep + exchange(send, "tp", 1)
    in_keep, in_got = ctx_second(in_keep, in_got)
    up, up_far = ctx_third(up_keep, up_got)
    in_got, up_far, far_out = together([in_got, up_far, far_out], part)
    outs = jnp.stack([own_out, far_out])
    got_outs = swap(outs, "tp", 1)
    up = join_bit(up, up_far, bit1)
    part = part + lax.ppermute(
        part.astype(BF16), both,
        [(g * 4 + s, g * 4 + (s ^ 2)) for g in range(4) for s in range(4) if s // 2 != g // 2],
    ).astype(F32)
    part = part.astype(BF16)
    moved = lax.ppermute(
        part, both,
        [(g * 4 + s, (g ^ 2) * 4 + s) for g in range(4) for s in range(4) if s // 2 == g // 2],
    )
    held = jnp.where(y == z // 2, part, moved)
    inside, in_far = ctx_third(in_keep, in_got)
    inside = join_bit(inside, in_far, bit1)
    shard_up = join_bit(up, swap(up, "ctx", 1), bit0).astype(F32)
    outputs = spread(outs, got_outs)
    moved = after(swap(held, "ctx", 1), outputs, input_grad, shard_up)
    shard_in = join_bit(inside, swap(inside, "ctx", 1), bit0).astype(F32)
    mine = jnp.where(c == bit0, held, moved)
    theirs = jnp.where(c == bit0, moved, held)
    shard_qkv = join_bit(mine, swap(theirs, "tp", 1), c).astype(F32)
    shard_out = shard_in[hidden_cut:]
    shard_in = shard_in[:hidden_cut]

    got = swap(sums, "dp", 1, 2) if pair else None
    sums = sums + after(got, *lin) if pair else lax.psum(sums, "dp")
    sums = sums + after(swap(sums, "ctx", 1), input_own)
    sums = sums + after(swap(sums, "ctx", 2), held)

    return (
        outputs,
        input_grad,
        shard_qkv[:head_cols].T,
        shard_qkv[head_cols : 2 * head_cols].T,
        shard_qkv[2 * head_cols :].T,
        shard_out,
        shard_in.T,
        shard_up,
        sums[0],
        sums[1],
        sums[2],
        sums[3],
    )


def solution(mesh):
    tokens = P("dp", "ctx", None)
    return jax.shard_map(
        functools.partial(per_device, mesh.shape["dp"]),
        mesh=mesh,
        in_specs=(
            tokens,
            P("dp", None),
            P("dp", "tp"),
            P("dp", "tp"),
            P("dp", "tp"),
            P("tp", "dp"),
            P("dp", "tp"),
            P("tp", "dp"),
            P(),
            P(),
            P(),
            P(),
            tokens,
        ),
        out_specs=(
            tokens,
            tokens,
            P("dp", "tp"),
            P("dp", "tp"),
            P("dp", "tp"),
            P("tp", "dp"),
            P("dp", "tp"),
            P("tp", "dp"),
            P(),
            P(),
            P(),
            P(),
        ),
        check_vma=False,
    )
```

```python
import functools
import math

import jax
import jax.numpy as jnp
from jax import lax
from jax.experimental import pallas as pl
from jax.experimental.pallas import tpu as pltpu
from jax.sharding import PartitionSpec as P

HEAD_DIM = 64
HALF = HEAD_DIM // 2
DOCS = 16
EPSILON = 1e-06
MASKED = -1e30
LOG2E = 1.0 / math.log(2.0)
F32 = jnp.float32
BF16 = jnp.bfloat16
GROUP = 4
KEY_BLOCKS = 8


def dot(left, right, left_dim, right_dim):
    return lax.dot_general(
        left, right, (((left_dim,), (right_dim,)), ((), ())), preferred_element_type=F32
    )


def swap(value, axis, k, size=GROUP):
    return lax.ppermute(value, axis, [(i, i ^ k) for i in range(size)])


def after(value, *others):
    return lax.optimization_barrier((value,) + others)[0]


def together(values, *others):
    there = [v for v in values if v is not None]
    there = iter(lax.optimization_barrier(tuple(there) + others)[: len(there)])
    return [None if v is None else next(there) for v in values]


def pick(stack, index):
    return lax.dynamic_index_in_dim(stack, index, 0, keepdims=False)


def split_bit(value, bit, axis=0):
    half = value.shape[axis] // 2
    keep = lax.dynamic_slice_in_dim(value, bit * half, half, axis)
    send = lax.dynamic_slice_in_dim(value, (1 - bit) * half, half, axis)
    return keep, send


def join_bit(own, other, bit, axis=0):
    low = jnp.where(bit == 0, own, other)
    high = jnp.where(bit == 0, other, own)
    return jnp.concatenate([low, high], axis)


def block_mask(base, span_ref, shape):
    key_index = base + lax.broadcasted_iota(jnp.int32, shape, 0)
    return (key_index >= span_ref[0, 0:1, :]) & (key_index < span_ref[0, 1:2, :])


def ones_below(value):
    return jnp.concatenate([value, jnp.ones((16, value.shape[1]), BF16)])


def minus_below(value, row):
    high = row.astype(BF16)
    rest = row - high.astype(F32)
    mid = rest.astype(BF16)
    last = (rest - mid.astype(F32)).astype(BF16)
    index = lax.broadcasted_iota(jnp.int32, (16, value.shape[1]), 0)
    parts = jnp.where(
        index == 0,
        high.astype(F32),
        jnp.where(index == 1, mid.astype(F32), jnp.where(index == 2, last.astype(F32), 0.0)),
    )
    return jnp.concatenate([value, (-parts).astype(BF16)])


def pair_flag(a, b):
    return jnp.where(a + b == 0, 0, jnp.where(a + b == 4, 2, 1))


def each_block(flags, i, work):
    def step(j, carry):
        flag = pair_flag(flags[i * KEY_BLOCKS + j], flags[i * KEY_BLOCKS + j + KEY_BLOCKS // 2])

        @pl.when(flag == 1)
        def _():
            work(j, True)

        @pl.when(flag == 2)
        def _():
            work(j, False)

        return carry

    lax.fori_loop(0, KEY_BLOCKS // 2, step, 0)


def attend_kernel(
    first, flags, bases, q_ref, k_ref, v_ref, span_ref, o_ref, lse_ref, m_s, q_s, acc_s
):
    i = first + pl.program_id(0)
    heads = q_ref.shape[1] // HEAD_DIM
    rows = q_ref.shape[2]
    parts = [slice(h * HEAD_DIM, (h + 1) * HEAD_DIM) for h in range(heads)]
    m_s[...] = jnp.full(m_s.shape, MASKED, F32)
    acc_s[...] = jnp.zeros(acc_s.shape, F32)

    def find_max(j, masked):
        both = (j, j + KEY_BLOCKS // 2)
        scores = [
            [dot(k_ref[b, part, :], q_ref[0, part, :], 0, 0) for part in parts] for b in both
        ]
        if masked:
            for n, b in enumerate(both):
                ok = block_mask(bases[b], span_ref, (rows, rows))
                scores[n] = [jnp.where(ok, s, MASKED) for s in scores[n]]
        tops = [
            [jnp.max(s.reshape(rows // 8, 8, rows), axis=0) for s in one] for one in scores
        ]
        for h in range(heads):
            m_s[h] = jnp.maximum(m_s[h], jnp.maximum(tops[0][h], tops[1][h]))

    each_block(flags, i, find_max)
    for h, part in enumerate(parts):
        top = jnp.max(m_s[h], axis=0, keepdims=True)
        lse_ref[0, h : h + 1, :] = top
        q_s[h] = minus_below(q_ref[0, part, :], top)

    def mix(j, masked):
        mixed = []
        for b in (j, j + KEY_BLOCKS // 2):
            probs = [
                jnp.exp2(dot(ones_below(k_ref[b, part, :]), q_s[h], 0, 0))
                for h, part in enumerate(parts)
            ]
            if masked:
                ok = block_mask(bases[b], span_ref, (rows, rows))
                probs = [jnp.where(ok, p, 0.0) for p in probs]
            mixed.append([
                dot(ones_below(v_ref[b, part, :]), p.astype(BF16), 1, 0)
                for part, p in zip(parts, probs)
            ])
        for h in range(heads):
            acc_s[h] += mixed[0][h] + mixed[1][h]

    each_block(flags, i, mix)
    for h, part in enumerate(parts):
        total = acc_s[h, HEAD_DIM : HEAD_DIM + 1, :]
        o_ref[0, part, :] = (acc_s[h, :HEAD_DIM, :] / total).astype(BF16)
        lse_ref[0, h : h + 1, :] = lse_ref[0, h : h + 1, :] + jnp.log2(total)


def attend(flags, bases, q, k, v, span, first, blocks):
    width, rows = q.shape[1:]
    heads = width // HEAD_DIM
    one = lambda shape: pl.BlockSpec((1,) + shape, lambda i, *_: (first + i, 0, 0))
    out = lambda shape: pl.BlockSpec((1,) + shape, lambda i, *_: (i, 0, 0))
    whole = pl.BlockSpec(k.shape, lambda i, *_: (0, 0, 0))
    return pl.pallas_call(
        functools.partial(attend_kernel, first),
        grid_spec=pltpu.PrefetchScalarGridSpec(
            num_scalar_prefetch=2,
            grid=(blocks,),
            in_specs=[one((width, rows)), whole, whole, one((2, rows))],
            out_specs=[out((width, rows)), out((heads, rows))],
            scratch_shapes=[
                pltpu.VMEM((heads, 8, rows), F32),
                pltpu.VMEM((heads, HEAD_DIM + 16, rows), BF16),
                pltpu.VMEM((heads, HEAD_DIM + 16, rows), F32),
            ],
        ),
        out_shape=[
            jax.ShapeDtypeStruct((blocks, width, rows), BF16),
            jax.ShapeDtypeStruct((blocks, heads, rows), F32),
        ],
        name="attend",
    )(flags, bases, q, k, v, span)


def attend_back_kernel(
    first, flags, bases, q_ref, k_ref, v_ref, span_ref, o_ref, d_ref, lse_ref, *refs
):
    if first:
        dq_ref, dk_s, dv_s, q_s, d_s = refs
    else:
        dk_in, dv_in, dq_ref, own_k_ref, own_v_ref, far_k_ref, far_v_ref = refs[:7]
        dk_s, dv_s, q_s, d_s = refs[7:]
    i = first + pl.program_id(0)
    heads = q_ref.shape[1] // HEAD_DIM
    parts = [slice(h * HEAD_DIM, (h + 1) * HEAD_DIM) for h in range(heads)]
    rows = q_ref.shape[2]

    @pl.when(pl.program_id(0) == 0)
    def _():
        dk_s[...] = jnp.zeros(dk_s.shape, F32) if first else dk_in[...]
        dv_s[...] = jnp.zeros(dv_s.shape, F32) if first else dv_in[...]

    dq_ref[...] = jnp.zeros(dq_ref.shape, F32)
    for h, part in enumerate(parts):
        grad = d_ref[0, part, :]
        delta = jnp.sum(o_ref[0, part, :].astype(F32) * grad.astype(F32), axis=0, keepdims=True)
        q_s[h] = minus_below(q_ref[0, part, :], lse_ref[0, h : h + 1, :])
        d_s[h] = minus_below(grad, delta)

    def work(j, masked):
        results = []
        for b in (j, j + KEY_BLOCKS // 2):
            keys = [k_ref[b, part, :] for part in parts]
            probs = [jnp.exp2(dot(ones_below(keys[h]), q_s[h], 0, 0)) for h in range(heads)]
            if masked:
                ok = block_mask(bases[b], span_ref, (rows, rows))
                probs = [jnp.where(ok, p, 0.0) for p in probs]
            shifted = [
                dot(ones_below(v_ref[b, part, :]), d_s[h], 0, 0) for h, part in enumerate(parts)
            ]
            scores = [(p * s).astype(BF16) for p, s in zip(probs, shifted)]
            d_v = [dot(d_ref[0, part, :], p.astype(BF16), 1, 1) for part, p in zip(parts, probs)]
            d_k = [dot(q_ref[0, part, :], s, 1, 1) for part, s in zip(parts, scores)]
            d_q = [dot(k, s, 1, 0) for k, s in zip(keys, scores)]
            results.append((d_v, d_k, d_q))
        for n, b in enumerate((j, j + KEY_BLOCKS // 2)):
            d_v, d_k, d_q = results[n]
            for h, part in enumerate(parts):
                dv_s[b, part, :] += d_v[h]
                dk_s[b, part, :] += d_k[h]
        for h, part in enumerate(parts):
            dq_ref[0, part, :] += results[0][2][h] + results[1][2][h]

    each_block(flags, i, work)
    if first:
        return

    @pl.when(pl.program_id(0) == pl.num_programs(0) - 1)
    def _():
        own = own_k_ref.shape[0]
        own_k_ref[...] = dk_s[:own]
        own_v_ref[...] = dv_s[:own]
        far_k_ref[...] = dk_s[own:].astype(BF16)
        far_v_ref[...] = dv_s[own:].astype(BF16)


def attend_back(flags, bases, q, k, v, span, o, grad, lse, first, sums):
    blocks = o.shape[0]
    width, rows = q.shape[1:]
    heads = width // HEAD_DIM
    at = lambda shape: pl.BlockSpec((1,) + shape, lambda i, *_: (first + i, 0, 0))
    one = lambda shape: pl.BlockSpec((1,) + shape, lambda i, *_: (i, 0, 0))
    whole = lambda n: pl.BlockSpec((n, width, rows), lambda i, *_: (0, 0, 0))
    total = jax.ShapeDtypeStruct(k.shape, F32)
    half = (k.shape[0] // 2, width, rows)
    out_shape = [jax.ShapeDtypeStruct((blocks, width, rows), F32)]
    out_specs = [one((width, rows))]
    scratch = [
        pltpu.VMEM((heads, HEAD_DIM + 16, rows), BF16),
        pltpu.VMEM((heads, HEAD_DIM + 16, rows), BF16),
    ]
    if first:
        out_shape += [total, total]
        out_specs += [whole(k.shape[0])] * 2
    else:
        out_shape += [jax.ShapeDtypeStruct(half, d) for d in (F32, F32, BF16, BF16)]
        out_specs += [whole(half[0])] * 4
        scratch = [pltpu.VMEM(k.shape, F32), pltpu.VMEM(k.shape, F32)] + scratch
    return pl.pallas_call(
        functools.partial(attend_back_kernel, first),
        grid_spec=pltpu.PrefetchScalarGridSpec(
            num_scalar_prefetch=2,
            grid=(blocks,),
            in_specs=[at((width, rows)), whole(k.shape[0]), whole(k.shape[0]), at((2, rows))]
            + [one((width, rows)), one((width, rows)), one((heads, rows))]
            + [whole(k.shape[0])] * len(sums),
            out_specs=out_specs,
            scratch_shapes=scratch,
        ),
        out_shape=out_shape,
        name="attend_back",
    )(flags, bases, q, k, v, span, o, grad, lse, *sums)


def rotate(value, cosines, sines):
    rows = value.shape[-1]
    parts = value.reshape(-1, 2, HALF, rows)
    lead, trail = parts[:, 0], parts[:, 1]
    return jnp.stack(
        [lead * cosines - trail * sines, trail * cosines + lead * sines], axis=1
    ).reshape(value.shape)


def norm_stats(rows):
    centre = jnp.mean(rows, axis=-1, keepdims=True)
    centred = rows - centre
    spread = jnp.mean(centred * centred, axis=-1, keepdims=True)
    scale = lax.rsqrt(spread + EPSILON)
    return centred * scale, scale


def norm_back(grad, normal, scale, gain):
    dn = grad * gain
    return scale * (
        dn
        - jnp.mean(dn, axis=-1, keepdims=True)
        - normal * jnp.mean(dn * normal, axis=-1, keepdims=True)
    )


def per_device(
    dp_size, inputs, segment_ids, w_query, w_key, w_value, w_output, w_inner, w_outer,
    gain_attn, shift_attn, gain_ffn, shift_ffn, cotangent,
):
    seqs, local_rows, width = inputs.shape
    rows = local_rows // 2
    x = lax.axis_index("dp")
    z = lax.axis_index("ctx")
    t = lax.axis_index("tp")
    y, c = t // 2, t % 2
    pair = dp_size == 2
    head_cols = w_query.shape[1]
    half_width = width // 2
    group_cols = 3 * head_cols

    def turn(value):
        if not pair:
            return value
        own, other = split_bit(value, x, value.ndim - 1)
        return jnp.concatenate([own, other], value.ndim - 1)

    def corner(value):
        flat = lambda d, s: d * GROUP + s
        return lax.ppermute(
            value, ("dp", "tp"),
            [(flat(d, s), flat(d ^ 1, s ^ 2)) for d in range(2) for s in range(GROUP)],
        )

    def across(local):
        if not pair:
            return None, None
        return swap(local, "dp", 1, 2), swap(local, "tp", 2)

    def gather(local, across_x, across_y, far_corner, axis):
        if not pair:
            near = lax.all_gather(local, "dp", axis=axis, tiled=True)
            return near, swap(near, "tp", 2)
        return (
            jnp.concatenate([local, across_x], axis),
            jnp.concatenate([across_y, far_corner], axis),
        )

    def exchange(value, axis, k, size=GROUP):
        return swap(value.astype(BF16), axis, k, size).astype(F32)

    def sum_dp(value):
        if not pair:
            return lax.psum_scatter(
                value.astype(BF16), "dp", scatter_dimension=value.ndim - 1, tiled=True
            ).astype(F32)
        return value[..., :half_width] + exchange(value[..., half_width:], "dp", 1, 2)

    bit0, bit1 = z % 2, z // 2

    def ctx_first(value):
        keep, send = split_bit(value, bit0)
        return keep, swap(send.astype(BF16), "ctx", 1)

    def ctx_second(keep, got):
        keep, send = split_bit(keep + got.astype(F32), bit1)
        return keep, swap(send.astype(BF16), "ctx", 2)

    def ctx_third(keep, got):
        keep = (keep + got.astype(F32)).astype(BF16)
        return keep, swap(keep, "ctx", 2)

    def own_tokens(value):
        return lax.dynamic_slice(value, (y, c * rows, 0), (1, rows, value.shape[2]))[0]

    own_in = turn(own_tokens(inputs))
    local = jnp.concatenate([w_query, w_key, w_value], 1)
    near, far = gather(local, *across(local), corner(local) if pair else None, 0)
    in_2 = swap(own_in, "ctx", 2)
    in_blocks = [own_in, swap(own_in, "ctx", 1), in_2, swap(in_2, "ctx", 1)]
    own_cot = turn(own_tokens(cotangent)).astype(F32)
    gain_a, shift_a, gain_f, shift_f = [
        turn(v)[None, :] for v in (gain_attn, shift_attn, gain_ffn, shift_ffn)
    ]
    def by_group(near, far):
        mine = jnp.stack([near, far])
        other = swap(mine, "tp", 1)
        stack = jnp.stack([mine[0], other[0], mine[1], other[1]])
        return [pick(stack, (t ^ z) ^ k) for k in range(GROUP)]

    w_qkv = by_group(near, far)
    mid = head_cols + w_outer.shape[0]
    down = jnp.concatenate([w_output, w_outer, w_inner.T])
    down = after(down, far)
    down_x, down_y = across(down)

    docs = pick(segment_ids, y)
    doc_names = jnp.arange(DOCS, dtype=jnp.int32)[:, None]
    doc_start = jnp.sum((docs[None, :] < doc_names).astype(jnp.int32), 1)
    doc_end = jnp.sum((docs[None, :] <= doc_names).astype(jnp.int32), 1)
    doc_blocks = docs.reshape(GROUP, 2, rows)
    order = jnp.stack([z ^ k for k in range(GROUP)])
    query_docs = jnp.stack([doc_blocks[z ^ k, c] for k in range(GROUP)])
    far_docs = jnp.stack([doc_blocks[z ^ k, 1 - c] for k in range(GROUP)])
    hot = query_docs[:, None, :] == doc_names[None]
    starts = jnp.sum(jnp.where(hot, doc_start[None, :, None], 0), 1)
    ends = jnp.sum(jnp.where(hot, doc_end[None, :, None], 0), 1)
    span = jnp.stack([starts, ends], 1)
    query_bases = (order * 2 + c) * rows
    bases = jnp.concatenate([query_bases, (order * 2 + 1 - c) * rows])
    key_docs = jnp.concatenate([query_docs, far_docs])
    key_low, key_high = key_docs[:, 0], key_docs[:, -1]
    low, high = query_docs[:, :1], query_docs[:, -1:]
    meets = (low <= key_high[None]) & (key_low[None] <= high)
    one_doc = (low == high) & (key_low == low) & (key_high == low)
    flags = jnp.where(meets, jnp.where(one_doc, 2, 1), 0).astype(jnp.int32).reshape(-1)
    position = (
        query_bases[:, None] + jnp.arange(rows, dtype=jnp.int32)[None] - starts
    ).astype(F32)
    theta = jnp.power(10000.0, -2.0 * jnp.arange(HALF, dtype=F32) / HEAD_DIM)
    angle = position[:, None, :] * theta[None, :, None]
    cosines, sines = jnp.cos(angle), jnp.sin(angle)

    factor = 1.0 / math.sqrt(HEAD_DIM)
    queries, keys, values = [], [], []
    for k, block in enumerate(in_blocks):
        lin = dot(w_qkv[0], block, 0, 1)
        query = rotate(lin[:head_cols], cosines[k], sines[k])
        queries.append((query * (factor * LOG2E)).astype(BF16))
        keys.append(rotate(lin[head_cols : 2 * head_cols], cosines[k], sines[k]).astype(BF16))
        values.append(lin[2 * head_cols :].astype(BF16))
    queries = jnp.stack(queries)
    own = jnp.stack(keys + values)
    got = swap(own, "tp", 1)
    keys = jnp.concatenate([own[:GROUP], got[:GROUP]])
    values = jnp.concatenate([own[GROUP:], got[GROUP:]])

    mixed_b, lse_b = attend(flags, bases, queries, keys, values, span, 2, 2)
    landed = [down_x, down_y] if pair else []
    mixed_0, lse_0 = attend(
        flags, after(bases, mixed_b, *landed), queries, keys, values, span, 0, 1
    )
    down_corner = None
    if pair:
        cut = down.shape[0] // 2
        late_x, late_y = after(down_x, mixed_b), after(down_y, mixed_b)
        low, high = swap(late_x[:cut], "tp", 2), swap(late_y[cut:], "dp", 1, 2)
        landed = [low, high]
    got_b = [swap(mixed_b[k], "ctx", k + 2) for k in range(2)]
    mixed_1, lse_1 = attend(
        flags, after(bases, mixed_0, *got_b, *landed), queries, keys, values, span, 1, 1
    )
    mixed_a, lse_a = jnp.concatenate([mixed_0, mixed_1]), jnp.concatenate([lse_0, lse_1])
    if pair:
        down_corner = jnp.concatenate([after(low, mixed_1), after(high, mixed_1)])
        down_x, down_y = after(down_x, mixed_1), after(down_y, mixed_1)
    near, far = gather(down, down_x, down_y, down_corner, 1)
    w_out = by_group(near[:head_cols], far[:head_cols])
    w_up = jnp.concatenate([near[head_cols:mid], far[head_cols:mid]])
    w_in = jnp.concatenate([near[mid:], far[mid:]])
    own_mixed = [mixed_0[0], swap(mixed_1[0], "ctx", 1)] + [after(g, mixed_1) for g in got_b]
    attended = functools.reduce(
        jnp.add, [dot(own_mixed[k], w_out[k], 0, 0) for k in (3, 2, 0, 1)]
    )

    normal_a, scale_a = norm_stats(own_in.astype(F32) + attended)
    first = normal_a * gain_a + shift_a
    first_own = first.astype(BF16)
    first_low = jnp.concatenate([first_own, swap(first_own, "tp", 1)])
    inner = dot(first_low, w_in, 1, 1)
    below = 0.5 * (1.0 + lax.erf(inner * math.sqrt(0.5)))
    density = jnp.exp(-0.5 * inner * inner) * (1.0 / math.sqrt(2.0 * math.pi))
    active = (inner * below).astype(BF16)
    slope = (below + inner * density).astype(BF16)
    active, slope = lax.optimization_barrier((active, slope))
    feed = dot(active, w_up, 1, 0)
    feed = feed[:rows] + exchange(feed[rows:], "tp", 1)
    normal_f, scale_f = norm_stats(first + feed)
    second = (normal_f * gain_f + shift_f).astype(BF16)

    def spread(own, got):
        quad = jnp.stack([own[0], got[0], own[1], got[1]])
        parts = [pick(quad, (k ^ t)) for k in range(GROUP)]
        return jnp.stack(parts).reshape(seqs, local_rows, width)

    d_second = norm_back(own_cot, normal_f, scale_f, gain_f)
    d_feed_own = d_second.astype(BF16)
    d_feed = jnp.concatenate([d_feed_own, swap(d_feed_own, "tp", 1)])
    hidden_cut = active.shape[1] // 2
    up_cut, in_cut = hidden_cut // 2, hidden_cut * 2 // 3

    def pieces(left, right, cut):
        part = lambda lo, hi: dot(left[:, lo:hi], right, 0, 0)
        near_low, far_low = part(0, cut), part(hidden_cut, hidden_cut + cut)
        near_high = part(cut, hidden_cut)
        far_high = part(hidden_cut + cut, 2 * hidden_cut)
        return near_low, far_low, near_high, far_high

    def send_dp(high):
        return swap(high[:, half_width:].astype(BF16), "dp", 1, 2) if pair else None

    def keep_dp(high, got):
        if pair:
            return high[:, :half_width] + got.astype(F32)
        return sum_dp(high)

    up = pieces(active, d_feed, up_cut)
    up_high = jnp.concatenate([up[2], up[3]])
    up_got = (swap(up[1].astype(BF16), "tp", 2), send_dp(up_high))
    d_inner = (dot(d_feed, w_up, 1, 1) * slope).astype(BF16)
    hidden = dot(d_inner, w_in, 1, 0)
    d_first = d_second + hidden[:rows] + exchange(hidden[rows:], "tp", 1)
    d_resid = norm_back(d_first, normal_a, scale_a, gain_a)
    d_attended = d_resid.astype(BF16)

    sent = [dot(w_out[k], d_attended, 1, 1).astype(BF16) for k in range(GROUP)]
    sent = list(lax.optimization_barrier(tuple(sent)))
    d_mixed = [sent[0]] + [swap(sent[k], "ctx", k) for k in range(1, GROUP)]

    late_first = after(first_low, *sent)
    inside = pieces(d_inner, late_first, in_cut)
    late_resid = after(d_attended, *sent)
    grad_out = jnp.stack([dot(own_mixed[k], late_resid, 1, 0) for k in range(GROUP)])
    ordered = [pick(grad_out, (t ^ z) ^ k) for k in range(GROUP)]
    got = exchange(jnp.stack([ordered[1], ordered[3]]), "tp", 1)
    out_near, out_far = ordered[0] + got[0], ordered[2] + got[1]
    in_high = jnp.concatenate([inside[2], out_near, inside[3], out_far])
    in_got = (swap(inside[1].astype(BF16), "tp", 2), send_dp(in_high))

    def second_stage(near_low, high, got_low, got_high, *others):
        got_low = after(got_low, *others)
        low = near_low + got_low.astype(F32)
        high = keep_dp(high, after(got_high, *others) if pair else None)
        cut = high.shape[0] // 2
        high, far = high[:cut], high[cut:]
        return low, high, send_dp(low), swap(far.astype(BF16), "tp", 2)

    def last_stage(low, high, got_low, got_high, *others):
        if others:
            got_low, got_high = together([got_low, got_high], *others)
        low = keep_dp(low, got_low)
        return jnp.concatenate([low, high + got_high.astype(F32)])

    up_low, up_high, *up_got = second_stage(up[0], up_high, *up_got, *sent)
    dq_b, sum_k, sum_v = attend_back(
        flags, after(bases, up_low, up_high), queries, keys, values, span, mixed_b,
        jnp.stack(d_mixed[2:]), lse_b, 2, (),
    )
    turn_q = lambda v, k: rotate(v * factor, cosines[k], -sines[k]).astype(BF16)
    lin_q = [None, None, turn_q(dq_b[0], 2), turn_q(dq_b[1], 3)]
    got_q = [None, None, swap(lin_q[2], "ctx", 2), swap(lin_q[3], "ctx", 3)]
    own_out = turn(second)
    up_got = together(up_got, dq_b)
    up = last_stage(up_low, up_high, *up_got)
    up_keep, up_got = ctx_first(up)
    in_low, in_high, *in_got = second_stage(inside[0], in_high, *in_got, dq_b)

    sums = jnp.stack(
        [
            jnp.sum(d_first * normal_a, 0),
            jnp.sum(d_first, 0),
            jnp.sum(own_cot * normal_f, 0),
            jnp.sum(own_cot, 0),
        ]
    )
    sums = turn(sums)
    sums = sums + after(swap(sums, "tp", 1), dq_b)
    dq_a, d_key, d_value, sent_key, sent_value = attend_back(
        flags, after(bases, up_keep, in_low, in_high, lin_q[2], lin_q[3]), queries, keys, values,
        span, mixed_a, jnp.stack(d_mixed[:2]), lse_a, 0, (sum_k, sum_v),
    )
    mark = dq_a
    lin_q[:2] = [turn_q(dq_a[0], 0), turn_q(dq_a[1], 1)]
    sums = sums + after(swap(sums, "tp", 2), mark)
    sibling = exchange(jnp.stack([sent_key, sent_value]), "tp", 1)
    got_q = [None, None] + together(got_q[2:], mark)
    far_out = swap(after(own_out, mark, sent_key), "tp", 2)
    up_keep, up_got = ctx_second(up_keep, after(up_got, mark))
    inside = last_stage(in_low, in_high, *in_got, mark)
    d_key = d_key + sibling[0]
    d_value = d_value + sibling[1]
    lin_kv = [
        jnp.concatenate(
            [
                rotate(d_key[k] * (1.0 / LOG2E), cosines[k], -sines[k]).astype(BF16),
                d_value[k].astype(BF16),
            ]
        )
        for k in range(GROUP)
    ]
    lin = [jnp.concatenate([lin_q[k], lin_kv[k]]) for k in range(GROUP)]
    in_keep, in_got = ctx_first(after(inside, *lin))
    grad_qkv = functools.reduce(
        jnp.add, [dot(lin[k], in_blocks[k], 1, 0) for k in range(GROUP)]
    )
    part = sum_dp(grad_qkv)
    arrived = [swap(lin[1], "ctx", 1)] + [swap(lin_kv[k], "ctx", k) for k in (2, 3)]
    *arrived, up_got, in_got = together([*arrived, up_got, in_got], grad_qkv.astype(BF16))
    received = [(lin[0], None), (arrived[0], None), (got_q[2], arrived[1]), (got_q[3], arrived[2])]
    through = []
    for k, (one, two) in enumerate(received):
        through.append(dot(one, w_qkv[k][:, : one.shape[0]], 0, 1))
        if two is not None:
            through.append(dot(two, w_qkv[k][:, one.shape[0] :], 0, 1))
    through = functools.reduce(jnp.add, through)
    input_own = (d_resid + through).astype(BF16)


    both = ("ctx", "tp")
    keep, send = split_bit(part, c)
    part = keep + exchange(send, "tp", 1)
    in_keep, in_got = ctx_second(in_keep, in_got)
    up, up_far = ctx_third(up_keep, up_got)
    in_got, up_far, far_out = together([in_got, up_far, far_out], part)
    outs = jnp.stack([own_out, far_out])
    got_outs = swap(outs, "tp", 1)
    up = join_bit(up, up_far, bit1)
    part = part + lax.ppermute(
        part.astype(BF16), both,
        [(g * 4 + s, g * 4 + (s ^ 2)) for g in range(4) for s in range(4) if s // 2 != g // 2],
    ).astype(F32)
    part = part.astype(BF16)
    in_grad = after(turn(input_own), part)
    in_grad = jnp.stack([in_grad, swap(in_grad, "tp", 2)])
    input_grad = spread(in_grad, swap(in_grad, "tp", 1))
    moved = lax.ppermute(
        part, both,
        [(g * 4 + s, (g ^ 2) * 4 + s) for g in range(4) for s in range(4) if s // 2 == g // 2],
    )
    held = jnp.where(y == z // 2, part, moved)
    inside, in_far = ctx_third(in_keep, in_got)
    inside = join_bit(inside, in_far, bit1)
    shard_up = join_bit(up, swap(up, "ctx", 1), bit0).astype(F32)
    outputs = spread(outs, got_outs)
    moved = after(swap(held, "ctx", 1), outputs, input_grad, shard_up)
    shard_in = join_bit(inside, swap(inside, "ctx", 1), bit0).astype(F32)
    mine = jnp.where(c == bit0, held, moved)
    theirs = jnp.where(c == bit0, moved, held)
    shard_qkv = join_bit(mine, swap(theirs, "tp", 1), c).astype(F32)
    shard_out = shard_in[hidden_cut:]
    shard_in = shard_in[:hidden_cut]

    got = swap(sums, "dp", 1, 2) if pair else None
    sums = sums + after(got, *lin) if pair else lax.psum(sums, "dp")
    sums = sums + after(swap(sums, "ctx", 1), input_own)
    sums = sums + after(swap(sums, "ctx", 2), held)

    return (
        outputs,
        input_grad,
        shard_qkv[:head_cols].T,
        shard_qkv[head_cols : 2 * head_cols].T,
        shard_qkv[2 * head_cols :].T,
        shard_out,
        shard_in.T,
        shard_up,
        sums[0],
        sums[1],
        sums[2],
        sums[3],
    )


def solution(mesh):
    tokens = P("dp", "ctx", None)
    return jax.shard_map(
        functools.partial(per_device, mesh.shape["dp"]),
        mesh=mesh,
        in_specs=(
            tokens,
            P("dp", None),
            P("dp", "tp"),
            P("dp", "tp"),
            P("dp", "tp"),
            P("tp", "dp"),
            P("dp", "tp"),
            P("tp", "dp"),
            P(),
            P(),
            P(),
            P(),
            tokens,
        ),
        out_specs=(
            tokens,
            tokens,
            P("dp", "tp"),
            P("dp", "tp"),
            P("dp", "tp"),
            P("tp", "dp"),
            P("dp", "tp"),
            P("tp", "dp"),
            P(),
            P(),
            P(),
            P(),
        ),
        check_vma=False,
    )
```
